32 devices in a mesh: section: 2 (over core), dp: 4 (over z), mp: 4 (over y, x).
Axes of the slice: x: 2, y: 2, z: 4, core: 2. Of those that a mesh axis runs over, the one named last changes fastest.
Arguments:
- images: float32 [24, 256, 48], P('dp'), may hold values from -1 to 1
- noise: float32 [24, 256, 48], P('dp'), may hold values from -6 to 6
- labels: int32 [24], P('dp'), may hold values from 0 to 999
- drop_mask: int32 [24], P('dp'), may hold values 0 or 1
- step_count: int32 [1], replicated, may hold values from 2 to 20
- qkv_weight: float32 [2, 768, 2304], P('section', 'dp', 'mp'), may hold values from -0.21875 to 0.21875
- attn_out_weight: float32 [2, 768, 768], P('section', 'mp', 'dp'), may hold values from -0.875 to 0.875
- up_weight: float32 [2, 768, 3072], P('section', 'dp', 'mp'), may hold values from -0.21875 to 0.21875
- down_weight: float32 [2, 3072, 768], P('section', 'mp', 'dp'), may hold values from -0.109375 to 0.109375
- head_weight: float32 [2, 768, 96], P('section', 'dp'), may hold values from -0.109375 to 0.109375
- embed_table: float32 [2, 1305, 768], P('section', None, 'dp'), may hold values from -1.2 to 1.2
- gains: float32 [2, 3, 768], P('section', None, 'dp'), may hold values from 0.5 to 1.5
- qkv_first: float32 [2, 768, 2304], P('section', 'dp', 'mp'), may hold values from -5.664445e-05 to 5.664445e-05
- attn_out_first: float32 [2, 768, 768], P('section', 'mp', 'dp'), may hold values from -5.664445e-05 to 5.664445e-05
- up_first: float32 [2, 768, 3072], P('section', 'dp', 'mp'), may hold values from -5.664445e-05 to 5.664445e-05
- down_first: float32 [2, 3072, 768], P('section', 'mp', 'dp'), may hold values from -5.664445e-05 to 5.664445e-05
- head_first: float32 [2, 768, 96], P('section', 'dp'), may hold values from -5.664445e-05 to 5.664445e-05
- embed_first: float32 [2, 1305, 768], P('section', None, 'dp'), may hold values from -5.664445e-05 to 5.664445e-05
- gains_first: float32 [2, 3, 768], P('section', None, 'dp'), may hold values from -5.664445e-05 to 5.664445e-05
- qkv_second: float32 [2, 768, 2304], P('section', 'dp', 'mp'), may hold values from 8.561198e-10 to 3.4179688e-09
- attn_out_second: float32 [2, 768, 768], P('section', 'mp', 'dp'), may hold values from 8.561198e-10 to 3.4179688e-09
- up_second: float32 [2, 768, 3072], P('section', 'dp', 'mp'), may hold values from 2.1158854e-10 to 8.626302e-10
- down_second: float32 [2, 3072, 768], P('section', 'mp', 'dp'), may hold values from 8.561198e-10 to 3.4179688e-09
- head_second: float32 [2, 768, 96], P('section', 'dp'), may hold values from 8.561198e-10 to 3.4179688e-09
- embed_second: float32 [2, 1305, 768], P('section', None, 'dp'), may hold values from 8.561198e-10 to 3.4179688e-09
- gains_second: float32 [2, 3, 768], P('section', None, 'dp'), may hold values from 8.561198e-10 to 3.4179688e-09
Outputs:
- loss: float32 [], replicated
- grad_norm: float32 [], replicated
- qkv_new: float32 [2, 768, 2304], P('section', 'dp', 'mp')
- qkv_first_new: float32 [2, 768, 2304], P('section', 'dp', 'mp')
- qkv_second_new: float32 [2, 768, 2304], P('section', 'dp', 'mp')
- attn_out_new: float32 [2, 768, 768], P('section', 'mp', 'dp')
- attn_out_first_new: float32 [2, 768, 768], P('section', 'mp', 'dp')
- attn_out_second_new: float32 [2, 768, 768], P('section', 'mp', 'dp')
- up_new: float32 [2, 768, 3072], P('section', 'dp', 'mp')
- up_first_new: float32 [2, 768, 3072], P('section', 'dp', 'mp')
- up_second_new: float32 [2, 768, 3072], P('section', 'dp', 'mp')
- down_new: float32 [2, 3072, 768], P('section', 'mp', 'dp')
- down_first_new: float32 [2, 3072, 768], P('section', 'mp', 'dp')
- down_second_new: float32 [2, 3072, 768], P('section', 'mp', 'dp')
- head_new: float32 [2, 768, 96], P('section', 'dp')
- head_first_new: float32 [2, 768, 96], P('section', 'dp')
- head_second_new: float32 [2, 768, 96], P('section', 'dp')
- embed_new: float32 [2, 1305, 768], P('section', None, 'dp')
- embed_first_new: float32 [2, 1305, 768], P('section', None, 'dp')
- embed_second_new: float32 [2, 1305, 768], P('section', None, 'dp')
- gains_new: float32 [2, 3, 768], P('section', None, 'dp')
- gains_first_new: float32 [2, 3, 768], P('section', None, 'dp')
- gains_second_new: float32 [2, 3, 768], P('section', None, 'dp')
The draws below stay inside these ranges and needn't reach their ends.
All inputs are finite; a program needn't handle non-finite values. No bound on the sum of `drop_mask` on one device may be relied on, other than what follows from the above.
Results may differ from the reference program's by a relative error of at most 0.023.
Values may be sent and summed in bfloat16 or wider, within the bound.
No kernel may reach another device: no remote copies, remote signals or barrier semaphores. Data moves between devices by JAX's collectives and lax.ppermute only.
A program may use at most 192 MiB of HBM per device.

```python
import math
import jax
import jax.numpy as jnp
from jax import lax

D = 768
HEAD = 64
FF = 3072
PDIM = 48
PATCHES = 256
NCLASS = 1000
ROWS = 1305
IMG_DEV = 6
IMAGES = 24
N_DP = 4
N_MP = 4


def place_ends(drawn, own_key, low, largest):
    spot = [jax.random.randint(jax.random.fold_in(own_key, axis), (), 0, length) for axis, length in enumerate(drawn.shape)]
    widest = drawn.shape.index(max(drawn.shape))
    next_to = spot[:widest] + [(spot[widest] + 1) % drawn.shape[widest]] + spot[widest + 1:]
    return drawn.at[tuple(spot)].set(low).at[tuple(next_to)].set(largest)


def levels(key, extent, split, smallest, largest):
    def one(axis_at, shards_of):
        steps = jax.random.uniform(jax.random.fold_in(jax.random.fold_in(key, 6), axis_at), (shards_of,), jnp.float32, smallest / len(split), largest / len(split))
        return jnp.repeat(jnp.exp(steps), extent[axis_at] // shards_of).reshape((-1,) + (1,) * (len(extent) - axis_at - 1))

    level = one(*split[0])
    for cut in split[1:]:
        level = level * one(*cut)
    return level


def centred(stream_key, extent, scale, reach, shards=(), held_as=jnp.bfloat16):
    array = jax.random.normal(stream_key, extent, jnp.float32) * scale
    if len(shards) > 0:
        array = levels(stream_key, extent, shards, -0.22, 0.18) * array
    return jnp.clip(array, min=-reach, max=reach).astype(held_as)


def setup_inputs(seed: int = 0) -> dict:
    arg_keys = jax.random.split(jax.random.key(seed), 27)
    return {
        "images": jnp.clip(jax.random.uniform(arg_keys[0], (IMAGES, PATCHES, PDIM), jnp.float32, -1.0, 1.0) * levels(arg_keys[0], (IMAGES, PATCHES, PDIM), ((0, 4),), -0.4, 0.0), -1.0, 1.0),
        "noise": centred(arg_keys[1], (IMAGES, PATCHES, PDIM), 1.0, 6.0, ((0, 4),), jnp.float32),
        "labels": place_ends(jax.random.randint(arg_keys[2], (IMAGES,), 0, NCLASS), jax.random.fold_in(arg_keys[2], 1), 0, NCLASS - 1).astype(jnp.int32),
        "drop_mask": place_ends((jax.random.randint(arg_keys[3], (IMAGES,), 0, 10) < 1).astype(jnp.int32), jax.random.fold_in(arg_keys[3], 1), 0, 1),
        "step_count": jax.random.randint(arg_keys[4], (1,), 2, 21).astype(jnp.int32),
        "qkv_weight": centred(arg_keys[5], (2, D, 3 * D), D ** -0.5, 0.21875, ((0, 2), (1, 4), (2, 4)), jnp.float32),
        "attn_out_weight": centred(arg_keys[6], (2, D, D), (D // 16) ** -0.5, 0.875, ((0, 2), (1, 4), (2, 4)), jnp.float32),
        "up_weight": centred(arg_keys[7], (2, D, FF), D ** -0.5, 0.21875, ((0, 2), (1, 4), (2, 4)), jnp.float32),
        "down_weight": centred(arg_keys[8], (2, FF, D), FF ** -0.5, 0.109375, ((0, 2), (1, 4), (2, 4)), jnp.float32),
        "head_weight": centred(arg_keys[9], (2, D, 2 * PDIM), (4 * D) ** -0.5, 0.109375, ((0, 2), (1, 4)), jnp.float32),
        "embed_table": centred(arg_keys[10], (2, ROWS, D), 0.2, 1.2, ((0, 2), (2, 4)), jnp.float32),
        "gains": jnp.clip(1.0 + 0.1 * jax.random.normal(arg_keys[11], (2, 3, D), jnp.float32), 0.5, 1.5),
        "qkv_first": centred(arg_keys[12], (2, D, 3 * D), (0.00111 * (IMAGES * PATCHES) ** -0.5), 5.6644450523890555e-05, ((0, 2), (1, 4), (2, 4)), jnp.float32),
        "attn_out_first": centred(arg_keys[13], (2, D, D), (0.00111 * (IMAGES * PATCHES) ** -0.5), 5.6644450523890555e-05, ((0, 2), (1, 4), (2, 4)), jnp.float32),
        "up_first": centred(arg_keys[14], (2, D, FF), (0.00111 * (IMAGES * PATCHES) ** -0.5), 5.6644450523890555e-05, ((0, 2), (1, 4), (2, 4)), jnp.float32),
        "down_first": centred(arg_keys[15], (2, FF, D), (0.00111 * (IMAGES * PATCHES) ** -0.5), 5.6644450523890555e-05, ((0, 2), (1, 4), (2, 4)), jnp.float32),
        "head_first": centred(arg_keys[16], (2, D, 2 * PDIM), (0.00111 * (IMAGES * PATCHES) ** -0.5), 5.6644450523890555e-05, ((0, 2), (1, 4)), jnp.float32),
        "embed_first": centred(arg_keys[17], (2, ROWS, D), (0.00111 * (IMAGES * PATCHES) ** -0.5), 5.6644450523890555e-05, ((0, 2), (2, 4)), jnp.float32),
        "gains_first": centred(arg_keys[18], (2, 3, D), (0.00111 * (IMAGES * PATCHES) ** -0.5), 5.6644450523890555e-05, ((0, 2), (2, 4)), jnp.float32),
        "qkv_second": jnp.clip(jnp.exp(math.log(3.4179687968816097e-09) - 1.3843914 * jax.random.uniform(arg_keys[19], (2, D, 3 * D), jnp.float32) ** levels(arg_keys[19], (2, D, 3 * D), ((0, 2), (1, 4), (2, 4)), -0.2, 0.2)), 8.561197861745029e-10, 3.4179687968816097e-09),
        "attn_out_second": jnp.clip(jnp.exp(math.log(3.4179687968816097e-09) - 1.3843914 * jax.random.uniform(arg_keys[20], (2, D, D), jnp.float32) ** levels(arg_keys[20], (2, D, D), ((0, 2), (1, 4), (2, 4)), -0.2, 0.2)), 8.561197861745029e-10, 3.4179687968816097e-09),
        "up_second": jnp.clip(jnp.exp(math.log(8.626301895020561e-10) - 1.40534255 * jax.random.uniform(arg_keys[21], (2, D, FF), jnp.float32) ** levels(arg_keys[21], (2, D, FF), ((0, 2), (1, 4), (2, 4)), -0.2, 0.2)), 2.115885383568994e-10, 8.626301895020561e-10),
        "down_second": jnp.clip(jnp.exp(math.log(3.4179687968816097e-09) - 1.3843914 * jax.random.uniform(arg_keys[22], (2, FF, D), jnp.float32) ** levels(arg_keys[22], (2, FF, D), ((0, 2), (1, 4), (2, 4)), -0.2, 0.2)), 8.561197861745029e-10, 3.4179687968816097e-09),
        "head_second": jnp.clip(jnp.exp(math.log(3.4179687968816097e-09) - 1.3843914 * jax.random.uniform(arg_keys[23], (2, D, 2 * PDIM), jnp.float32) ** levels(arg_keys[23], (2, D, 2 * PDIM), ((0, 2), (1, 4)), -0.2, 0.2)), 8.561197861745029e-10, 3.4179687968816097e-09),
        "embed_second": jnp.clip(jnp.exp(math.log(3.4179687968816097e-09) - 1.3843914 * jax.random.uniform(arg_keys[24], (2, ROWS, D), jnp.float32) ** levels(arg_keys[24], (2, ROWS, D), ((0, 2), (2, 4)), -0.2, 0.2)), 8.561197861745029e-10, 3.4179687968816097e-09),
        "gains_second": jnp.clip(jnp.exp(math.log(3.4179687968816097e-09) - 1.3843914 * jax.random.uniform(arg_keys[25], (2, 3, D), jnp.float32) ** levels(arg_keys[25], (2, 3, D), ((0, 2), (2, 4)), -0.2, 0.2)), 8.561197861745029e-10, 3.4179687968816097e-09),
    }


@jax.custom_vjp
def low(v):
    return lax.optimization_barrier(v.astype(jnp.bfloat16)).astype(jnp.float32)

@jax.custom_vjp
def low_back(v):
    return v

def low_keep(v):
    return (low(v), None)

def low_pass(kept, grad):
    return (grad,)

def back_keep(v):
    return (v, None)

def back_low(kept, grad):
    return (low(grad),)
low.defvjp(low_keep, low_pass)
low_back.defvjp(back_keep, back_low)
ln_eps = 1e-06
pen_weight = 0.5
noise_scale = 0.1
beta_one = 0.9
beta_two = 0.95
adam_eps = 1e-08
learn_rate = 0.05
gain_rate = 0.4
decay_rate = 0.1
clip_scale = 0.01
highest = lax.Precision.HIGHEST

def layer_norm(values, gain_row):
    centered = values - lax.optimization_barrier(jnp.mean(values, -1, keepdims=True))
    return centered * lax.rsqrt(lax.optimization_barrier(jnp.mean(centered * centered, -1, keepdims=True)) + ln_eps) * gain_row

def masked_softmax(scores):
    positions = scores.shape[-1]
    causal = jnp.arange(positions)[:, None] >= jnp.arange(positions)[None, :]
    return jax.nn.softmax(jnp.where(causal, scores, -1e+30), axis=-1)

def couple(flipped, head_out):
    patch_dim = flipped.shape[-1]
    shift_vals = head_out[..., :patch_dim]
    log_scale = head_out[..., patch_dim:]
    zero_row = jnp.zeros_like(shift_vals[:, :1])
    prev_shift = jnp.concatenate([zero_row, shift_vals[:, :-1]], 1)
    prev_scale = jnp.concatenate([zero_row, log_scale[:, :-1]], 1)
    latent = (flipped - prev_shift) * jnp.exp(-prev_scale)
    used_scale = log_scale[:, :-1]
    return (latent, jnp.sum(used_scale + pen_weight * used_scale * used_scale))

def flow_block(weights, latent, section_idx, tag_rows):
    attn_in, attn_out, ffn_up, ffn_down, head_proj, embed_rows, gain_set = weights
    groups = N_MP
    batch_size, patches, patch_dim = latent.shape
    model_width = embed_rows.shape[1]
    flipped = latent[:, ::-1] if section_idx == 1 else latent
    embedded = low_back(jnp.einsum('bpc,cd->bpd', low(flipped), embed_rows[:patch_dim], precision=highest))
    class_count = embed_rows.shape[0] - patch_dim - patches
    onehot = (tag_rows[:, None] == jnp.arange(class_count)[None, :]).astype(jnp.float32)
    class_rows = jnp.dot(onehot, embed_rows[patch_dim + patches:], precision=highest)
    resid = embedded + embed_rows[patch_dim:patch_dim + patches][None] + class_rows[:, None]
    spread = low_back(jnp.broadcast_to(low(layer_norm(resid, gain_set[0])), (groups,) + resid.shape))
    projected = low(low_back(jnp.einsum('gbpd,dge->gbpe', spread, attn_in.reshape(model_width, groups, -1), precision=highest)))
    projected = projected.reshape(groups, batch_size, patches, -1, 3, HEAD)
    scale_inv = 1.0 / math.sqrt(HEAD)
    scores = low_back(jnp.einsum('gbqhe,gbkhe->gbhqk', projected[..., 0, :], projected[..., 1, :], precision=highest) * scale_inv)
    attn_probs = low(masked_softmax(scores))
    context = low(low_back(jnp.einsum('gbhqk,gbkhe->gbqhe', attn_probs, projected[..., 2, :], precision=highest)))
    context = context.reshape(groups, batch_size, patches, -1)
    partials = low(low_back(jnp.einsum('gbpe,ged->gbpd', context, attn_out.reshape(groups, -1, model_width), precision=highest)))
    resid = resid + lax.optimization_barrier(jnp.sum(partials, 0))
    spread = low_back(jnp.broadcast_to(low(layer_norm(resid, gain_set[1])), (groups,) + resid.shape))
    upper = low_back(jnp.einsum('gbpd,dgf->gbpf', spread, ffn_up.reshape(model_width, groups, -1), precision=highest))
    hidden = low(jax.nn.gelu(upper))
    partials = low(low_back(jnp.einsum('gbpf,gfd->gbpd', hidden, ffn_down.reshape(groups, -1, model_width), precision=highest)))
    resid = resid + lax.optimization_barrier(jnp.sum(partials, 0))
    final = low(layer_norm(resid, gain_set[2]))
    head_out = low_back(jnp.einsum('bpd,dc->bpc', final, head_proj, precision=highest))
    return couple(flipped, head_out)

def reference(images, noise, labels, drop_mask, step_count, qkv_weight, attn_out_weight, up_weight, down_weight, head_weight, embed_table, gains, qkv_first, attn_out_first, up_first, down_first, head_first, embed_first, gains_first, qkv_second, attn_out_second, up_second, down_second, head_second, embed_second, gains_second):
    masters = (qkv_weight, attn_out_weight, up_weight, down_weight, head_weight, embed_table, gains)
    firsts = (qkv_first, attn_out_first, up_first, down_first, head_first, embed_first, gains_first)
    seconds = (qkv_second, attn_out_second, up_second, down_second, head_second, embed_second, gains_second)
    patch_count = IMAGES * PATCHES
    inputs = (images + noise_scale * noise).reshape(N_DP, IMG_DEV, PATCHES, PDIM)
    tag_all = jnp.where(drop_mask == 1, NCLASS, labels).astype(jnp.int32).reshape(N_DP, IMG_DEV)

    def total_loss(params):
        lowered = tuple((low(array_in) for array_in in params))

        def one_group(carry, group):
            latent, group_tags = group
            summed = jnp.zeros((), jnp.float32)
            for section_idx in range(2):
                latent, log_term = flow_block(tuple((weight[section_idx] for weight in lowered)), latent, section_idx, group_tags)
                summed = summed + log_term
            return (carry + summed + 0.5 * jnp.sum(latent * latent), None)
        total, _ = lax.scan(jax.checkpoint(one_group), jnp.zeros((), jnp.float32), (inputs, tag_all))
        return total / patch_count
    loss_value, pullback = jax.vjp(total_loss, masters)
    grads = pullback(jnp.ones((), jnp.float32))[0]
    param_count = sum((master.size for master in masters))
    limit = clip_scale * math.sqrt(param_count / patch_count)
    grad_norm = jnp.sqrt(sum((jnp.sum(grad * grad) for grad in grads)))
    factor = jnp.minimum(1.0, limit / grad_norm)
    steps_done = step_count[0].astype(jnp.float32)
    fix_one = 1.0 - beta_one ** steps_done
    fix_two = 1.0 - beta_two ** steps_done
    results = [loss_value, grad_norm]
    for which_weight in range(7):
        clipped = grads[which_weight] * factor
        first_moment = beta_one * firsts[which_weight] + (1.0 - beta_one) * clipped
        second_moment = beta_two * seconds[which_weight] + (1.0 - beta_two) * clipped * clipped
        decay_here = decay_rate if which_weight < 6 else 0.0
        rate_here = learn_rate if which_weight < 6 else gain_rate
        fresh = masters[which_weight] - rate_here * (first_moment / fix_one / (jnp.sqrt(second_moment / fix_two) + adam_eps) + decay_here * masters[which_weight])
        results += [fresh, first_moment, second_moment]
    return tuple(results)
```

```python
import functools
import math

import jax
import jax.numpy as jnp
from jax import lax
from jax.experimental import pallas as pl
from jax.experimental.pallas import tpu as pltpu
from jax.sharding import PartitionSpec as P

HEAD = 64
PDIM = 48
NCLASS = 1000

ln_eps = 1e-06
pen_weight = 0.5
noise_scale = 0.1
beta_one = 0.9
beta_two = 0.95
adam_eps = 1e-08
learn_rate = 0.05
gain_rate = 0.4
decay_rate = 0.1
clip_scale = 0.01
highest = lax.Precision.HIGHEST
low = jnp.bfloat16
wide = jnp.float32


def dot(a, b, ca, cb):
    return lax.dot_general(a, b, (((ca,), (cb,)), ((), ())), preferred_element_type=wide)


def head_probs(q, k, mask):
    scores = dot(q, k, 1, 1) * (1.0 / math.sqrt(HEAD))
    scores = jnp.where(mask, scores, -1e30)
    raised = jnp.exp(scores - jnp.max(scores, -1, keepdims=True))
    return raised / jnp.sum(raised, -1, keepdims=True)


def causal_mask(size):
    return lax.broadcasted_iota(jnp.int32, (size, size), 0) >= lax.broadcasted_iota(
        jnp.int32, (size, size), 1
    )


def attend_kernel(heads, qkv_ref, ctx_ref):
    mask = causal_mask(qkv_ref.shape[0])
    for h in range(heads):
        at = h * 3 * HEAD
        q, k, v = (qkv_ref[:, at + j * HEAD : at + (j + 1) * HEAD] for j in range(3))
        probs = head_probs(q, k, mask)
        ctx_ref[:, h * HEAD : (h + 1) * HEAD] = dot(probs.astype(low), v, 1, 0).astype(low)


def attend_back_kernel(heads, qkv_ref, dctx_ref, out_ref):
    mask = causal_mask(qkv_ref.shape[0])
    inv = 1.0 / math.sqrt(HEAD)
    for h in range(heads):
        at = h * 3 * HEAD
        q, k, v = (qkv_ref[:, at + j * HEAD : at + (j + 1) * HEAD] for j in range(3))
        dctx = dctx_ref[:, h * HEAD : (h + 1) * HEAD]
        probs = head_probs(q, k, mask)
        dprobs = dot(dctx, v, 1, 1)
        dscores = probs * (dprobs - jnp.sum(dprobs * probs, -1, keepdims=True))
        dscores = dscores.astype(low)
        out_ref[:, at : at + HEAD] = (dot(dscores, k, 1, 0) * inv).astype(low)
        out_ref[:, at + HEAD : at + 2 * HEAD] = (dot(dscores, q, 0, 0) * inv).astype(low)
        out_ref[:, at + 2 * HEAD : at + 3 * HEAD] = dot(probs.astype(low), dctx, 0, 0).astype(low)


def attend(qkv):
    rows, width = qkv.shape
    heads = width // (3 * HEAD)
    return pl.pallas_call(
        functools.partial(attend_kernel, heads),
        out_shape=jax.ShapeDtypeStruct((rows, heads * HEAD), low),
        name="attend",
        cost_estimate=pl.CostEstimate(
            flops=4 * heads * rows * rows * HEAD,
            bytes_accessed=2 * rows * heads * HEAD * 4,
            transcendentals=heads * rows * rows,
        ),
    )(qkv)


def attend_back(qkv, dctx):
    rows, width = qkv.shape
    heads = width // (3 * HEAD)
    return pl.pallas_call(
        functools.partial(attend_back_kernel, heads),
        out_shape=jax.ShapeDtypeStruct((rows, width), low),
        name="attend_back",
        cost_estimate=pl.CostEstimate(
            flops=10 * heads * rows * rows * HEAD,
            bytes_accessed=2 * rows * heads * HEAD * 7,
            transcendentals=heads * rows * rows,
        ),
    )(qkv, dctx)


def mp_sum(parts):
    size = lax.axis_size("mp")
    if size != 4:
        return lax.psum(parts, "mp").astype(wide)
    half = parts.shape[0] // 2

    def swap(x, bit):
        return lax.ppermute(x, "mp", [(j, j ^ bit) for j in range(size)])

    one, two = parts[:half], parts[half:]
    one_in, two_in = swap(one, 1), swap(two, 2)
    one = (one.astype(wide) + one_in.astype(wide)).astype(low)
    two = (two.astype(wide) + two_in.astype(wide)).astype(low)
    one_in, two_in = swap(one, 2), swap(two, 1)
    return jnp.concatenate(
        [one.astype(wide) + one_in.astype(wide), two.astype(wide) + two_in.astype(wide)], 0
    )


def line_shift(x, block, by):
    count = lax.axis_size("dp")
    pairs = [
        (block * count + j, block * count + j + by) for j in range(count) if 0 <= j + by < count
    ]
    return lax.ppermute(x, ("section", "dp"), pairs)


def share(x, block):
    other = lax.ppermute(x, "section", [(block, 1 - block)])
    return jnp.where(lax.axis_index("section") == block, x, other)


def swap_cores(x):
    return lax.ppermute(x, "section", [(0, 1), (1, 0)])


def gather_rows(x, block):
    count = lax.axis_size("dp")
    if count > 4:
        return lax.all_gather(x, "dp", axis=0, tiled=True)
    me = lax.axis_index("dp")
    above, below = [x], [x]
    for _ in range(count - 1):
        above.append(line_shift(above[-1], block, -1))
        below.append(line_shift(below[-1], block, 1))
    pieces = []
    for j in range(count):
        options = [above[j - at] if j >= at else below[at - j] for at in range(count)]
        pieces.append(lax.select_n(me, *options) if count > 2 else jnp.where(me == 0, *options))
    return jnp.concatenate(pieces, 0)


def scatter_rows(total, block):
    count = lax.axis_size("dp")
    rows = total.shape[0] // count
    if count > 4:
        return lax.psum_scatter(
            total.astype(low), "dp", scatter_dimension=0, tiled=True
        ).astype(wide)
    me = lax.axis_index("dp")

    def piece(at):
        return lax.dynamic_slice_in_dim(total, jnp.clip(at, 0, count - 1) * rows, rows, 0)

    down_in = up_in = None
    for step in range(count - 1):
        to_down = piece(count - 1 - step + me)
        to_up = piece(step - (count - 1) + me)
        if step > 0:
            to_down = to_down + down_in.astype(wide)
            to_up = to_up + up_in.astype(wide)
        down_in = line_shift(to_down.astype(low), block, 1)
        up_in = line_shift(to_up.astype(low), block, -1)
    return piece(me) + down_in.astype(wide) + up_in.astype(wide)


def to_owner(total, block):
    other = lax.ppermute(total.astype(low), "section", [(1 - block, block)])
    return total + other.astype(wide)


def ring_shift(x, by):
    count = lax.axis_size("dp")
    if by % count == 0:
        return x
    return lax.ppermute(x, "dp", [(j, (j + by) % count) for j in range(count)])


def everywhere_sum(vector):
    for axis in ("section", "mp", "dp"):
        size = lax.axis_size(axis)
        if size & (size - 1):
            vector = lax.psum(vector, axis)
            continue
        bit = 1
        while bit < size:
            vector = vector + lax.ppermute(vector, axis, [(j, j ^ bit) for j in range(size)])
            bit *= 2
    return vector


def class_rows_of(tags, table):
    count = lax.axis_size("dp")
    me = lax.axis_index("dp")
    width = table.shape[1]
    if count > 4:
        every = lax.all_gather(tags, "dp", axis=0, tiled=True)
        picked = pick_rows(every, table)
        rows = lax.all_to_all(
            picked.reshape(count, tags.shape[0], width), "dp", 0, 0, tiled=False
        )
        return jnp.concatenate([rows[j] for j in range(count)], 1), every
    by_offset = [ring_shift(tags, -d) for d in range(count)]
    back = [ring_shift(pick_rows(by_offset[d], table), d) for d in range(count)]
    pieces = []
    for j in range(count):
        options = [back[(at - j) % count] for at in range(count)]
        pieces.append(lax.select_n(me, *options) if count > 2 else jnp.where(me == 0, *options))
    return jnp.concatenate(pieces, 1), by_offset


def one_hot(tags, classes):
    return tags[:, None] == lax.broadcasted_iota(jnp.int32, (tags.shape[0], classes), 1)


def pick_rows(tags, table):
    return dot(one_hot(tags, table.shape[0]).astype(low), table, 1, 0).astype(low)


def class_gradient(sums, tag_sets, classes):
    count = lax.axis_size("dp")
    me = lax.axis_index("dp")
    width = sums.shape[1] // count
    if count > 4:
        images = sums.shape[0]
        parts = sums.reshape(images, count, width).transpose(1, 0, 2)
        got = lax.all_to_all(parts, "dp", 0, 0, tiled=False).reshape(count * images, width)
        tags = tag_sets
    else:
        got, tags = [], []
        for d in range(count):
            at = lax.rem(me + d, count) * width
            got.append(ring_shift(lax.dynamic_slice_in_dim(sums, at, width, 1), d))
            tags.append(tag_sets[(-d) % count])
        got, tags = jnp.concatenate(got, 0), jnp.concatenate(tags, 0)
    return lax.dot_general(
        one_hot(tags, classes).astype(wide),
        got,
        (((0,), (0,)), ((), ())),
        precision=highest,
        preferred_element_type=wide,
    )


def norm_parts(h):
    centered = h - jnp.mean(h, -1, keepdims=True)
    inv = lax.rsqrt(jnp.mean(centered * centered, -1, keepdims=True) + ln_eps)
    return centered * inv, inv


def norm_back(dout, gain, n, inv):
    dn = dout * gain
    dh = inv * (dn - jnp.mean(dn, -1, keepdims=True) - n * jnp.mean(dn * n, -1, keepdims=True))
    return dh, jnp.sum(dout * n, 0)


def shifted(x):
    return jnp.concatenate([jnp.zeros_like(x[:1]), x[:-1]], 0)


def unshifted(x):
    return jnp.concatenate([x[1:], jnp.zeros_like(x[:1])], 0)


def block_forward(block, latents, class_rows, w):
    saved = []
    first = []
    for u, class_row in zip(latents, class_rows):
        f = u[::-1] if block == 1 else u
        f_low = f.astype(low)
        h0 = dot(f_low, w["patch"], 1, 0) + w["position"] + class_row[None].astype(wide)
        n, inv = norm_parts(h0)
        a1 = (n * w["gains"][0]).astype(low)
        qkv = dot(a1, w["qkv"], 1, 0).astype(low)
        ctx = attend(qkv)
        part = dot(ctx, w["out_t"], 1, 1).astype(low)
        saved.append(dict(f=f, f_low=f_low, n1=n, inv1=inv, a1=a1, qkv=qkv, ctx=ctx))
        first.append((h0, mp_sum(part)))
    second = []
    for (h0, total), kept in zip(first, saved):
        h1 = h0 + total
        n, inv = norm_parts(h1)
        a2 = (n * w["gains"][1]).astype(low)
        upper = dot(a2, w["up"], 1, 0)
        hidden = jax.nn.gelu(upper).astype(low)
        part = dot(hidden, w["down_t"], 1, 1).astype(low)
        kept.update(n2=n, inv2=inv, a2=a2, upper=upper, hidden=hidden)
        second.append((h1, mp_sum(part)))
    outs = []
    terms = 0.0
    for (h1, total), kept in zip(second, saved):
        h2 = h1 + total
        n, inv = norm_parts(h2)
        a3 = (n * w["gains"][2]).astype(low)
        y = dot(a3, w["head"], 1, 0)
        shift, scale = y[:, :PDIM], y[:, PDIM:]
        z = (kept["f"] - shifted(shift)) * jnp.exp(-shifted(scale))
        used = scale[:-1]
        terms = terms + jnp.sum(used + pen_weight * used * used)
        kept.update(n3=n, inv3=inv, a3=a3, scale=scale, z=z)
        outs.append(z)
    return outs, terms, saved


def block_backward(block, grads_z, saved, w, patch_count):
    total = {}

    def add(name, value):
        total[name] = total[name] + value if name in total else value

    first = []
    for gz, kept in zip(grads_z, saved):
        scale, z = kept["scale"], kept["z"]
        df = gz * jnp.exp(-shifted(scale))
        inner = jnp.where(
            lax.broadcasted_iota(jnp.int32, scale.shape, 0) < scale.shape[0] - 1,
            (1.0 + 2.0 * pen_weight * scale) / patch_count,
            0.0,
        )
        dy = jnp.concatenate([unshifted(-df), inner + unshifted(-gz * z)], 1).astype(low)
        add("head", dot(kept["a3"], dy, 0, 0))
        dh2, dgain = norm_back(dot(dy, w["head"], 1, 1), w["gains"][2], kept["n3"], kept["inv3"])
        add("gain2", dgain)
        dh2_low = dh2.astype(low)
        dhidden = dot(dh2_low, w["down_t"], 1, 0)
        dupper = jax.vjp(jax.nn.gelu, kept["upper"])[1](dhidden)[0].astype(low)
        part = dot(dupper, w["up"], 1, 1).astype(low)
        first.append((df, dh2, mp_sum(part)))
        add("down_t", dot(dh2_low, kept["hidden"], 0, 0))
        add("up", dot(kept["a2"], dupper, 0, 0))
    second = []
    for (df, dh2, da2), kept in zip(first, saved):
        dh, dgain = norm_back(da2, w["gains"][1], kept["n2"], kept["inv2"])
        add("gain1", dgain)
        dh1 = dh2 + dh
        dh1_low = dh1.astype(low)
        dctx = dot(dh1_low, w["out_t"], 1, 0).astype(low)
        dqkv = attend_back(kept["qkv"], dctx)
        part = dot(dqkv, w["qkv"], 1, 1).astype(low)
        second.append((df, dh1, mp_sum(part)))
        add("out_t", dot(dh1_low, kept["ctx"], 0, 0))
        add("qkv", dot(kept["a1"], dqkv, 0, 0))
    back = []
    sums = []
    for (df, dh1, da1), kept in zip(second, saved):
        dh, dgain = norm_back(da1, w["gains"][0], kept["n1"], kept["inv1"])
        add("gain0", dgain)
        dh0 = dh1 + dh
        dh0_low = dh0.astype(low)
        add("patch_t", dot(dh0_low, kept["f_low"], 0, 0))
        add("position", dh0)
        sums.append(jnp.sum(dh0, 0))
        df = df + dot(dh0_low, w["patch"], 1, 1)
        back.append(df[::-1] if block == 1 else df)
    return back, total, jnp.stack(sums, 0)


def pad_columns(x, width):
    return jnp.pad(x, ((0, 0), (0, width - x.shape[1])))


def up_to(width):
    return -(-width // 128) * 128


def local(
    images,
    noise,
    labels,
    drop_mask,
    step_count,
    qkv_weight,
    attn_out_weight,
    up_weight,
    down_weight,
    head_weight,
    embed_table,
    gains,
    qkv_first,
    attn_out_first,
    up_first,
    down_first,
    head_first,
    embed_first,
    gains_first,
    qkv_second,
    attn_out_second,
    up_second,
    down_second,
    head_second,
    embed_second,
    gains_second,
):
    masters = (qkv_weight, attn_out_weight, up_weight, down_weight, head_weight, embed_table, gains)
    firsts = (qkv_first, attn_out_first, up_first, down_first, head_first, embed_first, gains_first)
    seconds = (
        qkv_second,
        attn_out_second,
        up_second,
        down_second,
        head_second,
        embed_second,
        gains_second,
    )
    section = lax.axis_index("section")
    n_dp = lax.axis_size("dp")
    n_mp = lax.axis_size("mp")
    here, patches = images.shape[0], images.shape[1]
    mine = here // 2
    patch_count = here * n_dp * patches
    fixed_rows = PDIM + patches
    classes = embed_table.shape[1] - fixed_rows

    qkv_s = qkv_weight[0].astype(low)
    out_s = attn_out_weight[0].astype(low).T
    up_s = up_weight[0].astype(low)
    down_s = down_weight[0].astype(low).T
    head_s = head_weight[0].astype(low)
    table_s = embed_table[0].astype(low)
    table_w = up_to(fixed_rows + 3)
    fixed_s = pad_columns(
        jnp.concatenate([table_s[:fixed_rows], gains[0].astype(low)], 0).T, table_w
    )
    packets = (
        jnp.concatenate([fixed_s, qkv_s], 1),
        jnp.concatenate([up_s, out_s], 1),
        jnp.concatenate([down_s, head_s], 1),
    )

    tags = jnp.where(drop_mask == 1, NCLASS, labels)
    rows_own, tag_sets = class_rows_of(tags, table_s[fixed_rows:])
    rows_other = swap_cores(rows_own)

    weights = []
    tie = None
    for block in range(2):
        got = []
        for packet in packets:
            if tie is not None:
                packet, tie = lax.optimization_barrier((packet, tie))
            got.append(share(gather_rows(packet, block), block))
        tie = got[1][:8]
        q_at, u_at = table_w, up_s.shape[1]
        fixed = got[0][:, : fixed_rows + 3].T
        weights.append(
            dict(
                qkv=got[0][:, q_at:],
                patch=fixed[:PDIM],
                position=fixed[PDIM:fixed_rows].astype(wide),
                gains=fixed[fixed_rows:].astype(wide),
                up=got[1][:, :u_at],
                out_t=got[1][:, u_at:],
                down_t=got[2][:, : down_s.shape[1]],
                head=got[2][:, down_s.shape[1] :],
            )
        )

    def own_images(x):
        return lax.dynamic_slice_in_dim(x, section * mine, mine, 0)

    inputs = own_images(images) + noise_scale * own_images(noise)
    latents = [inputs[k] for k in range(mine)]
    loss_part = 0.0
    kept = []
    for block in range(2):
        rows = own_images(jnp.where(section == block, rows_own, rows_other))
        latents, terms, saved = block_forward(
            block, latents, [rows[k] for k in range(mine)], weights[block]
        )
        loss_part = loss_part + terms
        kept.append(saved)
    loss_part = loss_part + 0.5 * sum(jnp.sum(z * z) for z in latents)

    grads_z = [z / patch_count for z in latents]
    scattered = [None, None]
    sums = [None, None]
    for block in (1, 0):
        grads_z, total, sums[block] = block_backward(
            block, grads_z, kept[block], weights[block], patch_count
        )
        fixed_t = jnp.concatenate(
            [
                total["patch_t"],
                total["position"].T,
                jnp.stack([total["gain0"], total["gain1"], total["gain2"]], 1),
            ],
            1,
        )
        grad_packets = (
            jnp.concatenate([total["down_t"], total["head"]], 1),
            jnp.concatenate([total["up"], total["out_t"]], 1),
            jnp.concatenate([pad_columns(fixed_t, table_w), total["qkv"]], 1),
        )
        scattered[block] = [scatter_rows(to_owner(p, block), block) for p in grad_packets]

    own = [jnp.where(section == 0, a, b) for a, b in zip(scattered[0], scattered[1])]
    u_at, d_at = up_s.shape[1], down_s.shape[1]
    sums_in = swap_cores(jnp.where(section == 0, sums[1], sums[0]))
    sums_own = jnp.where(section == 0, sums[0], sums[1])
    sums_all = jnp.where(
        section == 0,
        jnp.concatenate([sums_own, sums_in], 0),
        jnp.concatenate([sums_in, sums_own], 0),
    )
    fixed_grad = own[2][:, : fixed_rows + 3].T
    grads = (
        own[2][:, table_w:],
        own[1][:, u_at:].T,
        own[1][:, :u_at],
        own[0][:, :d_at].T,
        own[0][:, d_at:],
        jnp.concatenate(
            [fixed_grad[:fixed_rows], class_gradient(sums_all, tag_sets, classes)], 0
        ),
        fixed_grad[fixed_rows:],
    )

    squares = 0.0
    for which in range(7):
        weight_sq = jnp.sum(grads[which] * grads[which])
        squares = squares + (weight_sq if which < 4 else weight_sq / n_mp)
    summed = everywhere_sum(jnp.stack([squares, loss_part / (patch_count * n_mp)]))
    grad_norm = jnp.sqrt(summed[0])
    param_count = 2 * sum(
        masters[which].size * n_dp * (n_mp if which < 4 else 1) for which in range(7)
    )
    limit = clip_scale * math.sqrt(param_count / patch_count)
    factor = jnp.minimum(1.0, limit / grad_norm)
    steps_done = step_count[0].astype(wide)
    fix_one = 1.0 - beta_one**steps_done
    fix_two = 1.0 - beta_two**steps_done
    results = [summed[1], grad_norm]
    for which in range(7):
        clipped = grads[which][None] * factor
        first_moment = beta_one * firsts[which] + (1.0 - beta_one) * clipped
        second_moment = beta_two * seconds[which] + (1.0 - beta_two) * clipped * clipped
        decay_here = decay_rate if which < 6 else 0.0
        rate_here = learn_rate if which < 6 else gain_rate
        fresh = masters[which] - rate_here * (
            first_moment / fix_one / (jnp.sqrt(second_moment / fix_two) + adam_eps)
            + decay_here * masters[which]
        )
        results += [fresh, first_moment, second_moment]
    return tuple(results)


def solution(mesh):
    split_rows = P("section", "dp", "mp")
    split_columns = P("section", "mp", "dp")
    weights = (
        split_rows,
        split_columns,
        split_rows,
        split_columns,
        P("section", "dp", None),
        P("section", None, "dp"),
        P("section", None, "dp"),
    )
    return jax.shard_map(
        local,
        mesh=mesh,
        in_specs=(P("dp", None, None), P("dp", None, None), P("dp"), P("dp"), P()) + weights * 3,
        out_specs=(P(), P()) + tuple(spec for spec in weights for _ in range(3)),
        check_vma=False,
    )
```

```python
import functools
import math

import jax
import jax.numpy as jnp
from jax import lax
from jax.experimental import pallas as pl
from jax.experimental.pallas import tpu as pltpu
from jax.sharding import PartitionSpec as P

HEAD = 64
PDIM = 48
NCLASS = 1000
LANES = 128

ln_eps = 1e-06
pen_weight = 0.5
noise_scale = 0.1
beta_one = 0.9
beta_two = 0.95
adam_eps = 1e-08
learn_rate = 0.05
gain_rate = 0.4
decay_rate = 0.1
clip_scale = 0.01
gelu_c = math.sqrt(2.0 / math.pi)
gelu_a = 0.044715
low = jnp.bfloat16
wide = jnp.float32
ints = jnp.int32


def dot(a, b, ca, cb):
    return lax.dot_general(a, b, (((ca,), (cb,)), ((), ())), preferred_element_type=wide)


def iota(shape, dim):
    return lax.broadcasted_iota(ints, shape, dim)


def up_to(width):
    return -(-width // LANES) * LANES


def call(body, name, scalars, arrays, outs, flops=0, trans=0):
    nbytes = sum(a.size * a.dtype.itemsize for a in arrays)
    nbytes += sum(math.prod(s) * jnp.dtype(d).itemsize for s, d in outs)
    return pl.pallas_call(
        body,
        out_shape=[jax.ShapeDtypeStruct(s, d) for s, d in outs],
        in_specs=[pl.BlockSpec(memory_space=pltpu.SMEM)] * len(scalars)
        + [pl.BlockSpec(memory_space=pltpu.VMEM)] * len(arrays),
        name=name,
        cost_estimate=pl.CostEstimate(flops=flops, bytes_accessed=nbytes, transcendentals=trans),
    )(*scalars, *arrays)


def norm_parts(h):
    centered = h - jnp.mean(h, -1, keepdims=True)
    inv = lax.rsqrt(jnp.mean(centered * centered, -1, keepdims=True) + ln_eps)
    return centered * inv, inv


def norm_back(dout, gain, n, inv):
    dn = dout * gain
    dh = inv * (dn - jnp.mean(dn, -1, keepdims=True) - n * jnp.mean(dn * n, -1, keepdims=True))
    return dh, jnp.sum(dout * n, 0, keepdims=True)


def causal_mask(size, flip):
    query, key = iota((size, size), 0), iota((size, size), 1)
    return key >= query if flip else query >= key


def head_probs(q, k, mask):
    scores = dot(q, k, 1, 1) * (1.0 / math.sqrt(HEAD))
    scores = jnp.where(mask, scores, -1e30)
    raised = jnp.exp(scores - jnp.max(scores, -1, keepdims=True))
    return raised / jnp.sum(raised, -1, keepdims=True)


def prev_rows(x, flip):
    rows = x.shape[0]
    first = rows - 1 if flip else 0
    rolled = pltpu.roll(x, rows - 1 if flip else 1, 0)
    return jnp.where(iota(x.shape, 0) == first, 0.0, rolled)


def next_rows(x, flip):
    rows = x.shape[0]
    last = 0 if flip else rows - 1
    rolled = pltpu.roll(x, 1 if flip else rows - 1, 0)
    return jnp.where(iota(x.shape, 0) == last, 0.0, rolled)


def joined(one, one_in, two, two_in):
    return jnp.concatenate(
        [
            one[...].astype(wide) + one_in[...].astype(wide),
            two[...].astype(wide) + two_in[...].astype(wide),
        ],
        0,
    )


def put_halves(part, one, two):
    half = part.shape[0] // 2
    one[...] = part[:half].astype(low)
    two[...] = part[half:].astype(low)


class Plan:
    def __init__(self, patches, n_img, classes, d_head, d_qkv, d_out):
        self.fixed = PDIM + patches
        self.gain_at = self.fixed
        self.class_at = self.fixed + 8
        self.table_w = up_to(self.class_at + n_img)
        self.head_at = self.table_w
        self.out_at = self.head_at + up_to(d_head)
        self.qkv = d_qkv
        self.width = max(self.out_at + d_out, d_qkv)
        self.d_head = d_head
        self.d_out = d_out


def enter_kernel(plan, flip, img, f, pw, qw, gains, left, h0, a1, qkv, ctx, one, two):
    rows = f.shape[0]
    at, row = iota((rows, plan.table_w), 1), iota((rows, plan.table_w), 0)
    spot = (rows - 1 - row if flip else row) + PDIM
    picked = (at == spot) | (at == plan.class_at + img[0])
    base = picked.astype(wide)
    first = jnp.where(iota((rows, LANES), 1) < PDIM, f[...], base[:, :LANES])
    left[:, :LANES] = first.astype(low)
    left[:, LANES:] = base[:, LANES:].astype(low)
    h = dot(left[...], pw[:, : plan.table_w], 1, 1)
    h0[...] = h
    n, _ = norm_parts(h)
    a = (n * gains[0:1]).astype(low)
    a1[...] = a
    qkv[...] = dot(a, qw[:, : plan.qkv], 1, 0).astype(low)
    mask = causal_mask(rows, flip)
    for k in range(plan.d_out // HEAD):
        at = k * 3 * HEAD
        q, key, v = (qkv[:, at + j * HEAD : at + (j + 1) * HEAD] for j in range(3))
        probs = head_probs(q, key, mask)
        ctx[:, k * HEAD : (k + 1) * HEAD] = dot(probs.astype(low), v, 1, 0).astype(low)
    put_halves(dot(ctx[...], pw[:, plan.out_at : plan.out_at + plan.d_out], 1, 1), one, two)


def ff_kernel(h0, a, a_in, b, b_in, up, down_t, gains, h1, a2, upper, hidden, one, two):
    h = h0[...] + joined(a, a_in, b, b_in)
    h1[...] = h
    n, _ = norm_parts(h)
    x = (n * gains[1:2]).astype(low)
    a2[...] = x
    u = dot(x, up[...], 1, 0)
    upper[...] = u
    act = (0.5 * u * (1.0 + jnp.tanh(gelu_c * (u + gelu_a * u * u * u)))).astype(low)
    hidden[...] = act
    put_halves(dot(act, down_t[...], 1, 1), one, two)


def head_kernel(plan, flip, h1, a, a_in, b, b_in, f, pw, gains, h2, a3, scale, z, sums):
    rows = f.shape[0]
    h = h1[...] + joined(a, a_in, b, b_in)
    h2[...] = h
    n, _ = norm_parts(h)
    x = (n * gains[2:3]).astype(low)
    a3[...] = x
    y = dot(x, pw[:, plan.head_at : plan.head_at + LANES], 1, 0)
    here = iota(y.shape, 1) < PDIM
    shift = jnp.where(here, y, 0.0)
    sc = jnp.where(here, pltpu.roll(y, LANES - PDIM, 1), 0.0)
    scale[...] = sc
    out = (f[...] - prev_rows(shift, flip)) * jnp.exp(-prev_rows(sc, flip))
    z[...] = out
    used = iota(y.shape, 0) != (0 if flip else rows - 1)
    term = jnp.where(used, sc + pen_weight * sc * sc, 0.0)
    sums[0:1] = jnp.sum(term, 0, keepdims=True)
    sums[1:2] = jnp.sum(out * out, 0, keepdims=True)


def head_back_kernel(plan, flip, last, patch_count, *refs):
    if not last:
        gz_ref, *refs = refs
    z, scale, h2, upper, pw, up, down_t, gains, df, dy, dh2, dh2_low, dupper, one, two, dg = refs
    rows = z.shape[0]
    gz = z[...] / patch_count if last else gz_ref[...]
    sc = scale[...]
    d = gz * jnp.exp(-prev_rows(sc, flip))
    df[...] = d
    here = iota(sc.shape, 1) < PDIM
    used = (iota(sc.shape, 0) != (0 if flip else rows - 1)) & here
    inner = jnp.where(used, (1.0 + 2.0 * pen_weight * sc) / patch_count, 0.0)
    dscale = inner + next_rows(-gz * z[...], flip)
    dshift = next_rows(-d, flip)
    at = iota(sc.shape, 1)
    dout = jnp.where(here, dshift, pltpu.roll(dscale, PDIM, 1))
    dout = jnp.where(at < 2 * PDIM, dout, 0.0).astype(low)
    dy[...] = dout
    n, inv = norm_parts(h2[...])
    da3 = dot(dout, pw[:, plan.head_at : plan.head_at + LANES], 1, 1)
    dh, dgain = norm_back(da3, gains[2:3], n, inv)
    dg[...] = dgain
    dh2[...] = dh
    dh_low = dh.astype(low)
    dh2_low[...] = dh_low
    dhidden = dot(dh_low, down_t[...], 1, 0)
    u = upper[...]
    t = jnp.tanh(gelu_c * (u + gelu_a * u * u * u))
    slope = 0.5 * (1.0 + t) + 0.5 * u * (1.0 - t * t) * gelu_c * (1.0 + 3.0 * gelu_a * u * u)
    du = (dhidden * slope).astype(low)
    dupper[...] = du
    put_halves(dot(du, up[...], 1, 1), one, two)


def attend_back_kernel(
    plan, flip, dh2, a, a_in, b, b_in, h1, qkv, pw, qw, gains, dh1, dh1_low, dqkv, one, two, dg
):
    rows = dh2.shape[0]
    n, inv = norm_parts(h1[...])
    dh, dgain = norm_back(joined(a, a_in, b, b_in), gains[1:2], n, inv)
    dg[...] = dgain
    total = dh2[...] + dh
    dh1[...] = total
    t_low = total.astype(low)
    dh1_low[...] = t_low
    dctx_all = dot(t_low, pw[:, plan.out_at : plan.out_at + plan.d_out], 1, 0).astype(low)
    mask = causal_mask(rows, flip)
    inv_root = 1.0 / math.sqrt(HEAD)
    for k in range(plan.d_out // HEAD):
        at = k * 3 * HEAD
        q, key, v = (qkv[:, at + j * HEAD : at + (j + 1) * HEAD] for j in range(3))
        dctx = dctx_all[:, k * HEAD : (k + 1) * HEAD]
        probs = head_probs(q, key, mask)
        dprobs = dot(dctx, v, 1, 1)
        dscores = (probs * (dprobs - jnp.sum(dprobs * probs, -1, keepdims=True))).astype(low)
        dqkv[:, at : at + HEAD] = (dot(dscores, key, 1, 0) * inv_root).astype(low)
        dqkv[:, at + HEAD : at + 2 * HEAD] = (dot(dscores, q, 0, 0) * inv_root).astype(low)
        dqkv[:, at + 2 * HEAD : at + 3 * HEAD] = dot(probs.astype(low), dctx, 0, 0).astype(low)
    put_halves(dot(dqkv[...], qw[:, : plan.qkv], 1, 1), one, two)


def leave_back_kernel(plan, through, dh1, a, a_in, b, b_in, h0, gains, *refs):
    n, inv = norm_parts(h0[...])
    dh, dgain = norm_back(joined(a, a_in, b, b_in), gains[0:1], n, inv)
    if through:
        df, pw, dh0_low, dg, gz = refs
    else:
        dh0_low, dg = refs
    dg[...] = dgain
    total = (dh1[...] + dh).astype(low)
    dh0_low[...] = total
    if through:
        back = dot(total, pw[:, :LANES], 1, 0)
        gz[...] = df[...] + jnp.where(iota(back.shape, 1) < PDIM, back, 0.0)


def place(section, value, first, second, columns):
    @pl.when(section == 0)
    def _():
        first[:, columns] = value

    @pl.when(section == 1)
    def _():
        second[:, columns] = value


def ff_grad_kernel(count, section, *refs):
    a2, dupper, dh2, hidden = (refs[j * count : (j + 1) * count] for j in range(4))
    keep, send = refs[4 * count :]
    up = sum(dot(x[...], y[...], 0, 0) for x, y in zip(a2, dupper)).astype(low)
    place(section[0], up, keep, send, slice(None))
    down = sum(dot(x[...], y[...], 0, 0) for x, y in zip(dh2, hidden)).astype(low)
    place(section[0], down, send, keep, slice(None))


def attend_grad_kernel(plan, count, section, *refs):
    a1, dqkv, dh1, ctx, dh0, left, a3, dy = (refs[j * count : (j + 1) * count] for j in range(8))
    dgains, keep, send = refs[8 * count :]
    qkv = sum(dot(x[...], y[...], 0, 0) for x, y in zip(a1, dqkv)).astype(low)
    place(section[0], qkv, send, keep, slice(0, plan.qkv))
    if plan.width > plan.qkv:
        blank = jnp.zeros((qkv.shape[0], plan.width - plan.qkv), low)
        place(section[0], blank, send, keep, slice(plan.qkv, plan.width))
    out = sum(dot(x[...], y[...], 0, 0) for x, y in zip(dh1, ctx)).astype(low)
    place(section[0], out, keep, send, slice(plan.out_at, plan.out_at + plan.d_out))
    end = plan.out_at + plan.d_out
    if plan.width > end:
        blank = jnp.zeros((out.shape[0], plan.width - end), low)
        place(section[0], blank, keep, send, slice(end, plan.width))
    head = sum(dot(x[...], y[...], 0, 0) for x, y in zip(a3, dy)).astype(low)
    place(section[0], head, keep, send, slice(plan.head_at, plan.head_at + LANES))
    table = sum(dot(x[...], y[...], 0, 0) for x, y in zip(dh0, left))
    shape = (8, plan.table_w)
    spot = (iota(shape, 1) == plan.gain_at + iota(shape, 0)).astype(low)
    table = table + dot(dgains[...].astype(low), spot, 0, 0)
    place(section[0], table.astype(low), keep, send, slice(0, plan.table_w))


def square_kernel(plan, n_mp, gp, gq, fp, fq, spots, qkv, out, up, down, head, table, gains, sq):
    rows = gp.shape[0]
    g = gq[:, : plan.qkv].astype(wide)
    qkv[...] = g
    total = jnp.sum(g * g)
    turn = (iota((plan.d_out, plan.d_out), 0) == iota((plan.d_out, plan.d_out), 1)).astype(low)
    g = dot(turn, gp[:, plan.out_at : plan.out_at + plan.d_out], 1, 1)
    out[...] = g
    total = total + jnp.sum(g * g)
    for source, target in ((fp, up), (fq, down)):
        g = source[...].astype(wide)
        target[...] = g
        total = total + jnp.sum(g * g)
    g = gp[:, plan.head_at : plan.head_at + plan.d_head].astype(wide)
    head[...] = g
    copied = jnp.sum(g * g)
    packed = gp[:, : plan.table_w]
    width = table.shape[1]
    pick = (spots[...] == iota((plan.table_w, width), 1)).astype(low)
    g = dot(packed, pick, 1, 0)
    table[...] = g
    copied = copied + jnp.sum(g * g)
    shape = (8, plan.table_w)
    spot = (iota(shape, 1) == plan.gain_at + iota(shape, 0)) & (iota(shape, 0) < 3)
    g = dot(spot.astype(low), packed, 1, 1)
    gains[...] = g[:3]
    copied = copied + jnp.sum(g * g)
    sq[0, 0] = total + copied / n_mp


def adam_kernel(scalars, *refs):
    factor, fix_one, fix_two = scalars[0], scalars[1], scalars[2]
    ins, outs = refs[:28], refs[28:]
    for which in range(7):
        g, w, m, v = ins[4 * which : 4 * which + 4]
        w_out, m_out, v_out = outs[3 * which : 3 * which + 3]
        clipped = g[...] * factor
        first = beta_one * m[...] + (1.0 - beta_one) * clipped
        second = beta_two * v[...] + (1.0 - beta_two) * clipped * clipped
        decay = decay_rate if which < 6 else 0.0
        rate = learn_rate if which < 6 else gain_rate
        step = first / fix_one / (jnp.sqrt(second / fix_two) + adam_eps)
        w_out[...] = w[...] - rate * (step + decay * w[...])
        m_out[...] = first
        v_out[...] = second


def swap(x, axis, bit):
    return lax.ppermute(x, axis, [(j, j ^ bit) for j in range(lax.axis_size(axis))])


def swap_cores(x):
    return swap(x, "section", 1)


def mp_sum(one, two):
    if lax.axis_size("mp") != 4:
        one, two = lax.psum(one, "mp"), lax.psum(two, "mp")
        return one, jnp.zeros_like(one), two, jnp.zeros_like(two)
    one_in, two_in = swap(one, "mp", 1), swap(two, "mp", 2)
    one = (one.astype(wide) + one_in.astype(wide)).astype(low)
    two = (two.astype(wide) + two_in.astype(wide)).astype(low)
    return one, swap(one, "mp", 2), two, swap(two, "mp", 1)


def slots(x, axis):
    size = lax.axis_size(axis)
    if size > 4:
        return lax.all_gather(x, axis, axis=0)
    mine = lax.dynamic_update_slice_in_dim(
        jnp.zeros((size,) + x.shape, x.dtype), x[None], lax.axis_index(axis), 0
    )
    total = mine
    for by in range(1, size):
        total = total + lax.ppermute(mine, axis, [(j, (j + by) % size) for j in range(size)])
    return total


def everywhere_sum(vector):
    for axis in ("section", "mp", "dp"):
        vector = jnp.sum(slots(vector, axis), 0)
    return vector


def pad_columns(x, width):
    return jnp.pad(x, ((0, 0), (0, width - x.shape[1])))


def local(
    images,
    noise,
    labels,
    drop_mask,
    step_count,
    qkv_weight,
    attn_out_weight,
    up_weight,
    down_weight,
    head_weight,
    embed_table,
    gains,
    qkv_first,
    attn_out_first,
    up_first,
    down_first,
    head_first,
    embed_first,
    gains_first,
    qkv_second,
    attn_out_second,
    up_second,
    down_second,
    head_second,
    embed_second,
    gains_second,
):
    masters = (qkv_weight, attn_out_weight, up_weight, down_weight, head_weight, embed_table, gains)
    firsts = (qkv_first, attn_out_first, up_first, down_first, head_first, embed_first, gains_first)
    seconds = (
        qkv_second,
        attn_out_second,
        up_second,
        down_second,
        head_second,
        embed_second,
        gains_second,
    )
    section = lax.axis_index("section")
    n_dp = lax.axis_size("dp")
    n_mp = lax.axis_size("mp")
    here, patches = images.shape[0], images.shape[1]
    mine = here // 2
    n_img = here * n_dp
    patch_count = n_img * patches
    fixed = PDIM + patches
    classes = embed_table.shape[1] - fixed
    model = embed_table.shape[2] * n_dp
    hid = up_weight.shape[2]
    plan = Plan(
        patches,
        n_img,
        classes,
        head_weight.shape[2],
        qkv_weight.shape[2],
        attn_out_weight.shape[1],
    )
    core = section[None].astype(ints)

    tags = slots(jnp.where(drop_mask == 1, NCLASS, labels), "dp").reshape(n_img)
    table_t = embed_table[0].T.astype(low)
    ids = fixed + tags
    hot = (ids[:, None] == iota((n_img, fixed + classes), 1)).astype(low)
    class_t = dot(table_t, hot, 1, 1).astype(low)
    gains_t = pad_columns(gains[0].T.astype(low), 8)
    packed_p = jnp.concatenate(
        [
            pad_columns(jnp.concatenate([table_t[:, :fixed], gains_t, class_t], 1), plan.table_w),
            pad_columns(head_weight[0].astype(low), plan.out_at - plan.head_at),
            attn_out_weight[0].T.astype(low),
        ],
        1,
    )
    first_packet = (
        pad_columns(packed_p, plan.width),
        pad_columns(qkv_weight[0].astype(low), plan.width),
    )
    second_packet = (up_weight[0].astype(low), down_weight[0].T.astype(low))

    def spread(packet):
        p, q = packet
        moved = swap_cores(jnp.where(section == 0, q, p))
        return jnp.where(section == 0, p, moved), jnp.where(section == 0, moved, q)

    def gather(x):
        mine_full = lax.all_gather(x, "dp", axis=0, tiled=True)
        other = swap_cores(mine_full)
        return (
            jnp.where(section == 0, mine_full, other),
            jnp.where(section == 0, other, mine_full),
        )

    spread_first, spread_second = spread(first_packet), spread(second_packet)
    weights = []
    for block in range(2):
        pw, qw = gather(spread_first[block])
        up, down_t = gather(spread_second[block])
        shape = (8, plan.table_w)
        spot = (iota(shape, 1) == plan.gain_at + iota(shape, 0)) & (iota(shape, 0) < 3)
        rows = dot(spot.astype(low), pw[:, : plan.table_w], 1, 1)
        weights.append((pw, qw, up, down_t, rows))

    def own_images(x):
        return lax.dynamic_slice_in_dim(x, section * mine, mine, 0)

    inputs = own_images(images) + noise_scale * own_images(noise)
    inputs = jnp.pad(inputs, ((0, 0), (0, 0), (0, LANES - PDIM)))
    latents = [inputs[k] for k in range(mine)]
    first_image = lax.axis_index("dp") * here + section * mine
    half = (patches // 2, model)
    full = (patches, model)
    tile = (patches, LANES)
    mac = 2 * patches * model
    loss_part = 0.0
    kept = []
    for block in range(2):
        pw, qw, up, down_t, rows = weights[block]
        flip = block == 1
        saved = []
        for k in range(mine):
            left, h0, a1, qkv, ctx, one, two = call(
                functools.partial(enter_kernel, plan, flip),
                "enter",
                [(first_image + k)[None].astype(ints)],
                [latents[k], pw, qw, rows],
                [
                    ((patches, plan.table_w), low),
                    (full, wide),
                    (full, low),
                    ((patches, plan.qkv), low),
                    ((patches, plan.d_out), low),
                    (half, low),
                    (half, low),
                ],
                mac * (plan.table_w + plan.qkv + plan.d_out),
                patches * patches * 4,
            )
            saved.append(
                dict(f=latents[k], left=left, h0=h0, a1=a1, qkv=qkv, ctx=ctx, p=mp_sum(one, two))
            )
        for kept_k in saved:
            h1, a2, upper, hidden, one, two = call(
                ff_kernel,
                "ff",
                [],
                [kept_k["h0"], *kept_k["p"], up, down_t, rows],
                [
                    (full, wide),
                    (full, low),
                    ((patches, hid), wide),
                    ((patches, hid), low),
                    (half, low),
                    (half, low),
                ],
                mac * hid * 2,
                patches * hid,
            )
            kept_k.update(h1=h1, a2=a2, upper=upper, hidden=hidden, p=mp_sum(one, two))
        for kept_k in saved:
            h2, a3, scale, z, sums = call(
                functools.partial(head_kernel, plan, flip),
                "head",
                [],
                [kept_k["h1"], *kept_k["p"], kept_k["f"], pw, rows],
                [(full, wide), (full, low), (tile, wide), (tile, wide), ((2, LANES), wide)],
                mac * LANES,
                patches * LANES,
            )
            kept_k.update(h2=h2, a3=a3, scale=scale, z=z)
            loss_part = loss_part + jnp.sum(sums[0])
            if block == 1:
                loss_part = loss_part + 0.5 * jnp.sum(sums[1])
        latents = [kept_k["z"] for kept_k in saved]
        kept.append(saved)

    grads_z = [None] * mine
    scattered = [None, None]

    def scatter(pair):
        keep, send = pair
        other = swap_cores(send)
        both = (keep.astype(wide) + other.astype(wide)).astype(low)
        return lax.psum_scatter(both, "dp", scatter_dimension=0, tiled=True)

    for block in (1, 0):
        pw, qw, up, down_t, rows = weights[block]
        flip = block == 1
        saved = kept[block]
        for k in range(mine):
            s = saved[k]
            df, dy, dh2, dh2_low, dupper, one, two, dg2 = call(
                functools.partial(head_back_kernel, plan, flip, block == 1, float(patch_count)),
                "head_back",
                [],
                ([] if block == 1 else [grads_z[k]])
                + [s["z"], s["scale"], s["h2"], s["upper"], pw, up, down_t, rows],
                [
                    (tile, wide),
                    (tile, low),
                    (full, wide),
                    (full, low),
                    ((patches, hid), low),
                    (half, low),
                    (half, low),
                    ((1, model), wide),
                ],
                mac * (LANES + 2 * hid),
                patches * hid,
            )
            s.update(
                df=df, dy=dy, dh2=dh2, dh2_low=dh2_low, dupper=dupper, dg2=dg2, p=mp_sum(one, two)
            )
        ff_grads = call(
            functools.partial(ff_grad_kernel, mine),
            "ff_grad",
            [core],
            [s[name] for name in ("a2", "dupper", "dh2_low", "hidden") for s in saved],
            [((model, hid), low)] * 2,
            mac * hid * 2 * mine,
        )
        ff_scattered = scatter(ff_grads)
        for k in range(mine):
            s = saved[k]
            dh1, dh1_low, dqkv, one, two, dg1 = call(
                functools.partial(attend_back_kernel, plan, flip),
                "attend_back",
                [],
                [s["dh2"], *s["p"], s["h1"], s["qkv"], pw, qw, rows],
                [
                    (full, wide),
                    (full, low),
                    ((patches, plan.qkv), low),
                    (half, low),
                    (half, low),
                    ((1, model), wide),
                ],
                mac * (plan.d_out * 2 + plan.qkv),
                patches * patches * 4,
            )
            s.update(dh1=dh1, dh1_low=dh1_low, dqkv=dqkv, dg1=dg1, p=mp_sum(one, two))
        for k in range(mine):
            s = saved[k]
            outs = call(
                functools.partial(leave_back_kernel, plan, block == 1),
                "leave_back",
                [],
                [s["dh1"], *s["p"], s["h0"], rows] + ([s["df"], pw] if block == 1 else []),
                [(full, low), ((1, model), wide)] + ([(tile, wide)] if block == 1 else []),
                mac * LANES,
            )
            s.update(dh0=outs[0], dg0=outs[1])
            if block == 1:
                grads_z[k] = outs[2]
        dgains = jnp.concatenate(
            [sum(s[name] for s in saved) for name in ("dg0", "dg1", "dg2")]
            + [jnp.zeros((5, model), wide)],
            0,
        )
        names = ("a1", "dqkv", "dh1_low", "ctx", "dh0", "left", "a3", "dy")
        attend_grads = call(
            functools.partial(attend_grad_kernel, plan, mine),
            "attend_grad",
            [core],
            [s[name] for name in names for s in saved] + [dgains],
            [((model, plan.width), low)] * 2,
            mac * plan.width * 2 * mine,
        )
        scattered[block] = (scatter(attend_grads), ff_scattered)

    own = []
    for at in range(2):
        zero, one = scattered[0][at], scattered[1][at]
        moved = swap_cores(jnp.where(section == 0, one, zero))
        own.append(jnp.where(section == 0, zero, moved))
        own.append(jnp.where(section == 0, moved, one))

    spots = jnp.concatenate(
        [
            jnp.arange(fixed, dtype=ints),
            jnp.full((8,), -1, ints),
            ids.astype(ints),
            jnp.full((plan.table_w - plan.class_at - n_img,), -1, ints),
        ]
    )[:, None]

    def flat(x, which):
        return x[0].T if which in (3, 5) else x[0]

    shapes = [flat(w, which).shape for which, w in enumerate(masters)]
    *grads, squares = pl.pallas_call(
        functools.partial(square_kernel, plan, float(n_mp)),
        out_shape=[jax.ShapeDtypeStruct(s, wide) for s in shapes]
        + [jax.ShapeDtypeStruct((1, 1), wide)],
        out_specs=[pl.BlockSpec(memory_space=pltpu.VMEM)] * 7
        + [pl.BlockSpec(memory_space=pltpu.SMEM)],
        name="squares",
    )(own[0], own[1], own[2], own[3], spots)

    summed = everywhere_sum(jnp.stack([squares[0, 0], loss_part / (patch_count * n_mp)]))
    grad_norm = jnp.sqrt(summed[0])
    param_count = 2 * sum(
        masters[which].size * n_dp * (n_mp if which < 4 else 1) for which in range(7)
    )
    limit = clip_scale * math.sqrt(param_count / patch_count)
    factor = jnp.minimum(1.0, limit / grad_norm)
    steps_done = step_count[0].astype(wide)
    fix_one = 1.0 - beta_one**steps_done
    fix_two = 1.0 - beta_two**steps_done
    arrays = []
    for which in range(7):
        arrays.append(grads[which])
        arrays += [flat(x[which], which) for x in (masters, firsts, seconds)]
    fresh = call(
        adam_kernel,
        "adam",
        [jnp.stack([factor, fix_one, fix_two])],
        arrays,
        [(shapes[which], wide) for which in range(7) for _ in range(3)],
    )
    results = [summed[1], grad_norm]
    for at, x in enumerate(fresh):
        results.append((x.T if at // 3 in (3, 5) else x)[None])
    return tuple(results)


def solution(mesh):
    split_rows = P("section", "dp", "mp")
    split_columns = P("section", "mp", "dp")
    weights = (
        split_rows,
        split_columns,
        split_rows,
        split_columns,
        P("section", "dp", None),
        P("section", None, "dp"),
        P("section", None, "dp"),
    )
    return jax.shard_map(
        local,
        mesh=mesh,
        in_specs=(P("dp", None, None), P("dp", None, None), P("dp"), P("dp"), P()) + weights * 3,
        out_specs=(P(), P()) + tuple(spec for spec in weights for _ in range(3)),
        check_vma=False,
    )
```

```python
import functools
import math

import jax
import jax.numpy as jnp
from jax import lax
from jax.experimental import pallas as pl
from jax.experimental.pallas import tpu as pltpu
from jax.sharding import PartitionSpec as P

HEAD = 64
PDIM = 48
NCLASS = 1000
LANES = 128
GRANT = 14 << 20

ln_eps = 1e-06
pen_weight = 0.5
noise_scale = 0.1
beta_one = 0.9
beta_two = 0.95
adam_eps = 1e-08
learn_rate = 0.05
gain_rate = 0.4
decay_rate = 0.1
clip_scale = 0.01
gelu_c = math.sqrt(2.0 / math.pi)
gelu_a = 0.044715
low = jnp.bfloat16
wide = jnp.float32
ints = jnp.int32


def dot(a, b, ca, cb):
    return lax.dot_general(a, b, (((ca,), (cb,)), ((), ())), preferred_element_type=wide)


def iota(shape, dim):
    return lax.broadcasted_iota(ints, shape, dim)


def up_to(width):
    return -(-width // LANES) * LANES


def call(body, name, scalars, arrays, outs, flops=0, trans=0, after=(), near=True):
    nbytes = sum(a.size * a.dtype.itemsize for a in arrays)
    nbytes += sum(math.prod(s) * jnp.dtype(d).itemsize for s, d in outs)
    if near:
        arrays = [pltpu.with_memory_space_constraint(a, pltpu.VMEM) for a in arrays]
    count = len(scalars) + len(arrays)

    def kernel(*refs):
        body(*refs[:count], *refs[count + len(after) :])

    return pl.pallas_call(
        kernel,
        out_shape=[pltpu.VMEM(s, d) if near else jax.ShapeDtypeStruct(s, d) for s, d in outs],
        in_specs=[pl.BlockSpec(memory_space=pltpu.SMEM)] * len(scalars)
        + [pl.BlockSpec(memory_space=pltpu.VMEM)] * len(arrays)
        + [pl.BlockSpec(memory_space=pl.ANY)] * len(after),
        name=name,
        compiler_params=pltpu.CompilerParams(vmem_limit_bytes=GRANT) if near else None,
        cost_estimate=pl.CostEstimate(flops=flops, bytes_accessed=nbytes, transcendentals=trans),
    )(*scalars, *arrays, *after)


def gate(x, token):
    def kernel(x_ref, token_ref, out_ref):
        del x_ref, token_ref, out_ref

    return pl.pallas_call(
        kernel,
        out_shape=jax.ShapeDtypeStruct(x.shape, x.dtype),
        in_specs=[pl.BlockSpec(memory_space=pl.ANY)] * 2,
        out_specs=pl.BlockSpec(memory_space=pl.ANY),
        input_output_aliases={0: 0},
        name="gate",
    )(x, token)


def norm_parts(h):
    centered = h - jnp.mean(h, -1, keepdims=True)
    inv = lax.rsqrt(jnp.mean(centered * centered, -1, keepdims=True) + ln_eps)
    return centered * inv, inv


def norm_back(dout, gain, n, inv):
    dn = dout * gain
    dh = inv * (dn - jnp.mean(dn, -1, keepdims=True) - n * jnp.mean(dn * n, -1, keepdims=True))
    return dh, jnp.sum(dout * n, 0, keepdims=True)


def causal_mask(size, flip):
    query, key = iota((size, size), 0), iota((size, size), 1)
    return key >= query if flip else query >= key


def head_probs(q, k, mask):
    scores = dot(q, k, 1, 1) * (1.0 / math.sqrt(HEAD))
    scores = jnp.where(mask, scores, -1e30)
    raised = jnp.exp(scores - jnp.max(scores, -1, keepdims=True))
    return raised / jnp.sum(raised, -1, keepdims=True)


def prev_rows(x, flip):
    rows = x.shape[0]
    first = rows - 1 if flip else 0
    rolled = pltpu.roll(x, rows - 1 if flip else 1, 0)
    return jnp.where(iota(x.shape, 0) == first, 0.0, rolled)


def next_rows(x, flip):
    rows = x.shape[0]
    last = 0 if flip else rows - 1
    rolled = pltpu.roll(x, 1 if flip else rows - 1, 0)
    return jnp.where(iota(x.shape, 0) == last, 0.0, rolled)


def joined(a, a_in):
    return a[...].astype(wide) + a_in[...].astype(wide)


class Plan:
    def __init__(self, patches, n_img, classes, d_head, d_qkv, d_out):
        self.fixed = PDIM + patches
        self.gain_at = self.fixed
        self.class_at = self.fixed + 8
        self.table_w = up_to(self.class_at + n_img)
        self.head_at = self.table_w
        self.out_at = self.head_at + up_to(d_head)
        self.qkv_at = self.out_at + up_to(d_out)
        self.qkv = d_qkv
        self.width = self.qkv_at + up_to(d_qkv)
        self.d_head = d_head
        self.d_out = d_out


def enter_kernel(plan, flip, img, f, pw, gains, left, h0, a1, qkv, ctx, part):
    rows = f.shape[0]
    at, row = iota((rows, plan.table_w), 1), iota((rows, plan.table_w), 0)
    spot = (rows - 1 - row if flip else row) + PDIM
    picked = (at == spot) | (at == plan.class_at + img[0])
    base = picked.astype(wide)
    first = jnp.where(iota((rows, LANES), 1) < PDIM, f[...], base[:, :LANES])
    left[:, :LANES] = first.astype(low)
    left[:, LANES:] = base[:, LANES:].astype(low)
    h = dot(left[...], pw[:, : plan.table_w], 1, 1)
    h0[...] = h
    n, _ = norm_parts(h)
    a = (n * gains[0:1]).astype(low)
    a1[...] = a
    qkv[...] = dot(a, pw[:, plan.qkv_at : plan.qkv_at + plan.qkv], 1, 0).astype(low)
    mask = causal_mask(rows, flip)
    for k in range(plan.d_out // HEAD):
        at = k * 3 * HEAD
        q, key, v = (qkv[:, at + j * HEAD : at + (j + 1) * HEAD] for j in range(3))
        probs = head_probs(q, key, mask)
        ctx[:, k * HEAD : (k + 1) * HEAD] = dot(probs.astype(low), v, 1, 0).astype(low)
    part[...] = dot(ctx[...], pw[:, plan.out_at : plan.out_at + plan.d_out], 1, 1).astype(low)


def ff_kernel(h0, a, a_in, fw, gains, h1, a2, upper, hidden, part):
    hid = upper.shape[1]
    h = h0[...] + joined(a, a_in)
    h1[...] = h
    n, _ = norm_parts(h)
    x = (n * gains[1:2]).astype(low)
    a2[...] = x
    u = dot(x, fw[:, :hid], 1, 0)
    upper[...] = u
    act = (0.5 * u * (1.0 + jnp.tanh(gelu_c * (u + gelu_a * u * u * u)))).astype(low)
    hidden[...] = act
    part[...] = dot(act, fw[:, hid:], 1, 1).astype(low)


def head_kernel(plan, flip, h1, a, a_in, f, pw, gains, h2, a3, scale, z, sums):
    rows = f.shape[0]
    h = h1[...] + joined(a, a_in)
    h2[...] = h
    n, _ = norm_parts(h)
    x = (n * gains[2:3]).astype(low)
    a3[...] = x
    y = dot(x, pw[:, plan.head_at : plan.head_at + LANES], 1, 0)
    here = iota(y.shape, 1) < PDIM
    shift = jnp.where(here, y, 0.0)
    sc = jnp.where(here, pltpu.roll(y, LANES - PDIM, 1), 0.0)
    scale[...] = sc
    out = (f[...] - prev_rows(shift, flip)) * jnp.exp(-prev_rows(sc, flip))
    z[...] = out
    used = iota(y.shape, 0) != (0 if flip else rows - 1)
    term = jnp.where(used, sc + pen_weight * sc * sc, 0.0)
    sums[0:1] = jnp.sum(term, 0, keepdims=True)
    sums[1:2] = jnp.sum(out * out, 0, keepdims=True)


def head_back_kernel(plan, flip, last, patch_count, *refs):
    if not last:
        gz_ref, *refs = refs
    z, scale, h2, upper, pw, fw, gains, df, dy, dh2, dh2_low, dupper, part, dg = refs
    hid = upper.shape[1]
    rows = z.shape[0]
    gz = z[...] / patch_count if last else gz_ref[...]
    sc = scale[...]
    d = gz * jnp.exp(-prev_rows(sc, flip))
    df[...] = d
    here = iota(sc.shape, 1) < PDIM
    used = (iota(sc.shape, 0) != (0 if flip else rows - 1)) & here
    inner = jnp.where(used, (1.0 + 2.0 * pen_weight * sc) / patch_count, 0.0)
    dscale = inner + next_rows(-gz * z[...], flip)
    dshift = next_rows(-d, flip)
    at = iota(sc.shape, 1)
    dout = jnp.where(here, dshift, pltpu.roll(dscale, PDIM, 1))
    dout = jnp.where(at < 2 * PDIM, dout, 0.0).astype(low)
    dy[...] = dout
    n, inv = norm_parts(h2[...])
    da3 = dot(dout, pw[:, plan.head_at : plan.head_at + LANES], 1, 1)
    dh, dgain = norm_back(da3, gains[2:3], n, inv)
    dg[...] = dgain
    dh2[...] = dh
    dh_low = dh.astype(low)
    dh2_low[...] = dh_low
    dhidden = dot(dh_low, fw[:, hid:], 1, 0)
    u = upper[...]
    t = jnp.tanh(gelu_c * (u + gelu_a * u * u * u))
    slope = 0.5 * (1.0 + t) + 0.5 * u * (1.0 - t * t) * gelu_c * (1.0 + 3.0 * gelu_a * u * u)
    du = (dhidden * slope).astype(low)
    dupper[...] = du
    part[...] = dot(du, fw[:, :hid], 1, 1).astype(low)


def attend_back_kernel(
    plan, flip, dh2, a, a_in, h1, qkv, pw, gains, dh1, dh1_low, dqkv, part, dg
):
    rows = dh2.shape[0]
    n, inv = norm_parts(h1[...])
    dh, dgain = norm_back(joined(a, a_in), gains[1:2], n, inv)
    dg[...] = dgain
    total = dh2[...] + dh
    dh1[...] = total
    t_low = total.astype(low)
    dh1_low[...] = t_low
    dctx_all = dot(t_low, pw[:, plan.out_at : plan.out_at + plan.d_out], 1, 0).astype(low)
    mask = causal_mask(rows, flip)
    inv_root = 1.0 / math.sqrt(HEAD)
    for k in range(plan.d_out // HEAD):
        at = k * 3 * HEAD
        q, key, v = (qkv[:, at + j * HEAD : at + (j + 1) * HEAD] for j in range(3))
        dctx = dctx_all[:, k * HEAD : (k + 1) * HEAD]
        probs = head_probs(q, key, mask)
        dprobs = dot(dctx, v, 1, 1)
        dscores = (probs * (dprobs - jnp.sum(dprobs * probs, -1, keepdims=True))).astype(low)
        dqkv[:, at : at + HEAD] = (dot(dscores, key, 1, 0) * inv_root).astype(low)
        dqkv[:, at + HEAD : at + 2 * HEAD] = (dot(dscores, q, 0, 0) * inv_root).astype(low)
        dqkv[:, at + 2 * HEAD : at + 3 * HEAD] = dot(probs.astype(low), dctx, 0, 0).astype(low)
    part[...] = dot(dqkv[...], pw[:, plan.qkv_at : plan.qkv_at + plan.qkv], 1, 1).astype(low)


def leave_back_kernel(plan, through, dh1, a, a_in, h0, gains, *refs):
    n, inv = norm_parts(h0[...])
    dh, dgain = norm_back(joined(a, a_in), gains[0:1], n, inv)
    if through:
        df, pw, dh0_low, dg, gz = refs
    else:
        dh0_low, dg = refs
    dg[...] = dgain
    total = (dh1[...] + dh).astype(low)
    dh0_low[...] = total
    if through:
        back = dot(total, pw[:, :LANES], 1, 0)
        gz[...] = df[...] + jnp.where(iota(back.shape, 1) < PDIM, back, 0.0)


def place(value, keep, send, start):
    half, columns = value.shape[0] // 2, slice(start, start + value.shape[1])
    keep[:, columns] = value[:half]
    send[:, columns] = value[half:]


def ff_grad_kernel(count, *refs):
    a2, dupper, dh2, hidden = (refs[j * count : (j + 1) * count] for j in range(4))
    keep, send = refs[4 * count :]
    up = sum(dot(x[...], y[...], 0, 0) for x, y in zip(a2, dupper)).astype(low)
    place(up, keep, send, 0)
    down = sum(dot(x[...], y[...], 0, 0) for x, y in zip(dh2, hidden)).astype(low)
    place(down, keep, send, up.shape[1])


def attend_grad_kernel(plan, count, *refs):
    a1, dqkv, dh1, ctx, dh0, left, a3, dy = (refs[j * count : (j + 1) * count] for j in range(8))
    dgains, keep, send = refs[8 * count :]
    qkv = sum(dot(x[...], y[...], 0, 0) for x, y in zip(a1, dqkv)).astype(low)
    qkv = jnp.pad(qkv, ((0, 0), (0, plan.width - plan.qkv_at - plan.qkv)))
    place(qkv, keep, send, plan.qkv_at)
    out = sum(dot(x[...], y[...], 0, 0) for x, y in zip(dh1, ctx)).astype(low)
    out = jnp.pad(out, ((0, 0), (0, plan.qkv_at - plan.out_at - plan.d_out)))
    place(out, keep, send, plan.out_at)
    head = sum(dot(x[...], y[...], 0, 0) for x, y in zip(a3, dy)).astype(low)
    place(head, keep, send, plan.head_at)
    table = sum(dot(x[...], y[...], 0, 0) for x, y in zip(dh0, left))
    shape = (8, plan.table_w)
    spot = (iota(shape, 1) == plan.gain_at + iota(shape, 0)).astype(low)
    table = table + dot(dgains[...].astype(low), spot, 0, 0)
    place(table.astype(low), keep, send, 0)


def join_kernel(one, two, out):
    half = one.shape[0]
    out[:half] = one[...]
    out[half:] = two[...]


def square_kernel(plan, n_mp, gp, fp, spots, qkv, out, up, down, head, table, gains, sq):
    hid = up.shape[1]
    g = gp[:, plan.qkv_at : plan.qkv_at + plan.qkv].astype(wide)
    qkv[...] = g
    total = jnp.sum(g * g)
    turn = (iota((plan.d_out, plan.d_out), 0) == iota((plan.d_out, plan.d_out), 1)).astype(low)
    g = dot(turn, gp[:, plan.out_at : plan.out_at + plan.d_out], 1, 1)
    out[...] = g
    total = total + jnp.sum(g * g)
    for source, target in ((fp[:, :hid], up), (fp[:, hid:], down)):
        g = source.astype(wide)
        target[...] = g
        total = total + jnp.sum(g * g)
    g = gp[:, plan.head_at : plan.head_at + plan.d_head].astype(wide)
    head[...] = g
    copied = jnp.sum(g * g)
    packed = gp[:, : plan.table_w]
    width = table.shape[1]
    pick = (spots[...] == iota((plan.table_w, width), 1)).astype(low)
    g = dot(packed, pick, 1, 0)
    table[...] = g
    copied = copied + jnp.sum(g * g)
    shape = (8, plan.table_w)
    spot = (iota(shape, 1) == plan.gain_at + iota(shape, 0)) & (iota(shape, 0) < 3)
    g = dot(spot.astype(low), packed, 1, 1)
    gains[...] = g[:3]
    copied = copied + jnp.sum(g * g)
    sq[0, 0] = total + copied / n_mp


def adam_step(g, w, m, v, factor, fix_one, fix_two, rate, decay):
    clipped = g * factor
    first = beta_one * m + (1.0 - beta_one) * clipped
    second = beta_two * v + (1.0 - beta_two) * clipped * clipped
    step = first / fix_one / (jnp.sqrt(second / fix_two) + adam_eps)
    return w - rate * (step + decay * w), first, second


def adam_kernel(scalars, *refs):
    factor, fix_one, fix_two = scalars[0], scalars[1], scalars[2]
    ins, outs = refs[:24], refs[24:]
    for which in range(6):
        g, w, m, v = ins[4 * which : 4 * which + 4]
        w_out, m_out, v_out = outs[3 * which : 3 * which + 3]
        values = (g[...], w[...], m[...], v[...])
        w_out[...], m_out[...], v_out[...] = adam_step(
            *values, factor, fix_one, fix_two, learn_rate, decay_rate
        )


def swap(x, axis, bit):
    return lax.ppermute(x, axis, [(j, j ^ bit) for j in range(lax.axis_size(axis))])


def swap_cores(x):
    return swap(x, "section", 1)


def mp_sum(part, turn):
    if lax.axis_size("mp") != 4:
        part = lax.psum(part, "mp")
        return part, jnp.zeros_like(part)
    bits = (1, 2) if turn % 2 == 0 else (2, 1)
    part = (part.astype(wide) + swap(part, "mp", bits[0]).astype(wide)).astype(low)
    return part, swap(part, "mp", bits[1])


def slots(x, axis):
    size = lax.axis_size(axis)
    if size > 4:
        return lax.all_gather(x, axis, axis=0)
    mine = lax.dynamic_update_slice_in_dim(
        jnp.zeros((size,) + x.shape, x.dtype), x[None], lax.axis_index(axis), 0
    )
    total = mine
    for by in range(1, size):
        total = total + lax.ppermute(mine, axis, [(j, (j + by) % size) for j in range(size)])
    return total


def everywhere_sum(vector):
    for axis in ("section", "mp", "dp"):
        vector = jnp.sum(slots(vector, axis), 0)
    return vector


def pad_columns(x, width):
    return jnp.pad(x, ((0, 0), (0, width - x.shape[1])))


def local(
    images,
    noise,
    labels,
    drop_mask,
    step_count,
    qkv_weight,
    attn_out_weight,
    up_weight,
    down_weight,
    head_weight,
    embed_table,
    gains,
    qkv_first,
    attn_out_first,
    up_first,
    down_first,
    head_first,
    embed_first,
    gains_first,
    qkv_second,
    attn_out_second,
    up_second,
    down_second,
    head_second,
    embed_second,
    gains_second,
):
    masters = (qkv_weight, attn_out_weight, up_weight, down_weight, head_weight, embed_table, gains)
    firsts = (qkv_first, attn_out_first, up_first, down_first, head_first, embed_first, gains_first)
    seconds = (
        qkv_second,
        attn_out_second,
        up_second,
        down_second,
        head_second,
        embed_second,
        gains_second,
    )
    section = lax.axis_index("section")
    n_dp = lax.axis_size("dp")
    n_mp = lax.axis_size("mp")
    here, patches = images.shape[0], images.shape[1]
    mine = here // 2
    n_img = here * n_dp
    patch_count = n_img * patches
    fixed = PDIM + patches
    classes = embed_table.shape[1] - fixed
    model = embed_table.shape[2] * n_dp
    hid = up_weight.shape[2]
    plan = Plan(
        patches,
        n_img,
        classes,
        head_weight.shape[2],
        qkv_weight.shape[2],
        attn_out_weight.shape[1],
    )

    tags = slots(jnp.where(drop_mask == 1, NCLASS, labels), "dp").reshape(n_img)
    table_t = embed_table[0].T.astype(low)
    ids = fixed + tags
    hot = (ids[:, None] == iota((n_img, fixed + classes), 1)).astype(low)
    class_t = dot(table_t, hot, 1, 1).astype(low)
    gains_t = pad_columns(gains[0].T.astype(low), 8)
    packets = (
        jnp.concatenate(
            [
                pad_columns(
                    jnp.concatenate([table_t[:, :fixed], gains_t, class_t], 1), plan.table_w
                ),
                pad_columns(head_weight[0].astype(low), plan.out_at - plan.head_at),
                pad_columns(attn_out_weight[0].T.astype(low), plan.qkv_at - plan.out_at),
                pad_columns(qkv_weight[0].astype(low), plan.width - plan.qkv_at),
            ],
            1,
        ),
        jnp.concatenate([up_weight[0].astype(low), down_weight[0].T.astype(low)], 1),
    )

    def spread(packet):
        rows = packet.shape[0] // 2
        low_rows, high_rows = packet[:rows], packet[rows:]
        moved = swap_cores(jnp.where(section == 0, high_rows, low_rows))
        return jnp.where(section == 0, low_rows, moved), jnp.where(section == 0, moved, high_rows)

    spread_packets = [spread(packet) for packet in packets]

    def gather(packet, block, token=None):
        own_rows = lax.all_gather(spread_packets[packet][block], "dp", axis=0, tiled=True)
        if token is not None:
            own_rows = gate(own_rows, token)
        other = swap_cores(own_rows)
        rows, width = own_rows.shape
        return call(join_kernel, "join", [], [own_rows, other], [((2 * rows, width), low)])[0]

    def gain_rows(pw):
        shape = (8, plan.table_w)
        spot = (iota(shape, 1) == plan.gain_at + iota(shape, 0)) & (iota(shape, 0) < 3)
        return dot(spot.astype(low), pw[:, : plan.table_w], 1, 1)

    def own_images(x):
        return lax.dynamic_slice_in_dim(x, section * mine, mine, 0)

    inputs = own_images(images) + noise_scale * own_images(noise)
    inputs = jnp.pad(inputs, ((0, 0), (0, 0), (0, LANES - PDIM)))
    latents = [inputs[k] for k in range(mine)]
    first_image = lax.axis_index("dp") * here + section * mine
    full = (patches, model)
    tile = (patches, LANES)
    mac = 2 * patches * model
    loss_part = 0.0
    kept = []
    weights = []
    for block in range(2):
        pw = gather(0, block, kept[0][mine - 1]["p"][0] if block else None)
        rows = gain_rows(pw)
        flip = block == 1
        saved = []
        for k in range(mine):
            left, h0, a1, qkv, ctx, part = call(
                functools.partial(enter_kernel, plan, flip),
                "enter",
                [(first_image + k)[None].astype(ints)],
                [latents[k], pw, rows],
                [
                    ((patches, plan.table_w), low),
                    (full, wide),
                    (full, low),
                    ((patches, plan.qkv), low),
                    ((patches, plan.d_out), low),
                    (full, low),
                ],
                mac * (plan.table_w + plan.qkv + plan.d_out),
                patches * patches * 4,
            )
            saved.append(
                dict(f=latents[k], left=left, h0=h0, a1=a1, qkv=qkv, ctx=ctx, p=mp_sum(part, k))
            )
        fw = gather(1, block, part)
        weights.append((pw, fw, rows))
        for k, kept_k in enumerate(saved):
            h1, a2, upper, hidden, part = call(
                ff_kernel,
                "ff",
                [],
                [kept_k["h0"], *kept_k["p"], fw, rows],
                [
                    (full, wide),
                    (full, low),
                    ((patches, hid), wide),
                    ((patches, hid), low),
                    (full, low),
                ],
                mac * hid * 2,
                patches * hid,
            )
            kept_k.update(h1=h1, a2=a2, upper=upper, hidden=hidden, p=mp_sum(part, k))
        for kept_k in saved:
            h2, a3, scale, z, sums = call(
                functools.partial(head_kernel, plan, flip),
                "head",
                [],
                [kept_k["h1"], *kept_k["p"], kept_k["f"], pw, rows],
                [(full, wide), (full, low), (tile, wide), (tile, wide), ((2, LANES), wide)],
                mac * LANES,
                patches * LANES,
            )
            kept_k.update(h2=h2, a3=a3, scale=scale, z=z)
            loss_part = loss_part + jnp.sum(sums[0])
            if block == 1:
                loss_part = loss_part + 0.5 * jnp.sum(sums[1])
        latents = [kept_k["z"] for kept_k in saved]
        kept.append(saved)

    grads_z = [None] * mine
    scattered = [None, None]

    def scatter(pair):
        keep, send = pair
        other = swap_cores(send)
        both = (keep.astype(wide) + other.astype(wide)).astype(low)
        return lax.psum_scatter(both, "dp", scatter_dimension=0, tiled=True)

    for block in (1, 0):
        pw, fw, rows = weights[block]
        flip = block == 1
        saved = kept[block]
        for k in range(mine):
            s = saved[k]
            df, dy, dh2, dh2_low, dupper, part, dg2 = call(
                functools.partial(head_back_kernel, plan, flip, block == 1, float(patch_count)),
                "head_back",
                [],
                ([] if block == 1 else [grads_z[k]])
                + [s["z"], s["scale"], s["h2"], s["upper"], pw, fw, rows],
                [
                    (tile, wide),
                    (tile, low),
                    (full, wide),
                    (full, low),
                    ((patches, hid), low),
                    (full, low),
                    ((1, model), wide),
                ],
                mac * (LANES + 2 * hid),
                patches * hid,
            )
            s.update(
                df=df, dy=dy, dh2=dh2, dh2_low=dh2_low, dupper=dupper, dg2=dg2, p=mp_sum(part, k)
            )
        ff_grads = call(
            functools.partial(ff_grad_kernel, mine),
            "ff_grad",
            [],
            [s[name] for name in ("a2", "dupper", "dh2_low", "hidden") for s in saved],
            [((model // 2, 2 * hid), low)] * 2,
            mac * hid * 2 * mine,
            after=[] if block else [attend_grads[0]],
        )
        ff_scattered = scatter(ff_grads)
        for k in range(mine):
            s = saved[k]
            dh1, dh1_low, dqkv, part, dg1 = call(
                functools.partial(attend_back_kernel, plan, flip),
                "attend_back",
                [],
                [s["dh2"], *s["p"], s["h1"], s["qkv"], pw, rows],
                [
                    (full, wide),
                    (full, low),
                    ((patches, plan.qkv), low),
                    (full, low),
                    ((1, model), wide),
                ],
                mac * (plan.d_out * 2 + plan.qkv),
                patches * patches * 4,
            )
            s.update(dh1=dh1, dh1_low=dh1_low, dqkv=dqkv, dg1=dg1, p=mp_sum(part, k))
        for k in range(mine):
            s = saved[k]
            outs = call(
                functools.partial(leave_back_kernel, plan, block == 1),
                "leave_back",
                [],
                [s["dh1"], *s["p"], s["h0"], rows] + ([s["df"], pw] if block == 1 else []),
                [(full, low), ((1, model), wide)] + ([(tile, wide)] if block == 1 else []),
                mac * LANES,
            )
            s.update(dh0=outs[0], dg0=outs[1])
            if block == 1:
                grads_z[k] = outs[2]
        dgains = jnp.concatenate(
            [sum(s[name] for s in saved) for name in ("dg0", "dg1", "dg2")]
            + [jnp.zeros((5, model), wide)],
            0,
        )
        names = ("a1", "dqkv", "dh1_low", "ctx", "dh0", "left", "a3", "dy")
        attend_grads = call(
            functools.partial(attend_grad_kernel, plan, mine),
            "attend_grad",
            [],
            [s[name] for name in names for s in saved] + [dgains],
            [((model // 2, plan.width), low)] * 2,
            mac * plan.width * mine,
        )
        scattered[block] = (scatter(attend_grads), ff_scattered)

    own = []
    for at in range(2):
        zero, one = scattered[0][at], scattered[1][at]
        moved = swap_cores(jnp.where(section == 0, one, zero))
        own.append(
            jnp.where(
                section == 0,
                jnp.concatenate([zero, moved], 0),
                jnp.concatenate([moved, one], 0),
            )
        )

    spots = jnp.concatenate(
        [
            jnp.arange(fixed, dtype=ints),
            jnp.full((8,), -1, ints),
            ids.astype(ints),
            jnp.full((plan.table_w - plan.class_at - n_img,), -1, ints),
        ]
    )[:, None]

    def flat(x, which):
        return x[0].T if which in (3, 5) else x[0]

    shapes = [flat(w, which).shape for which, w in enumerate(masters)]
    *grads, squares = pl.pallas_call(
        functools.partial(square_kernel, plan, float(n_mp)),
        out_shape=[jax.ShapeDtypeStruct(s, wide) for s in shapes]
        + [jax.ShapeDtypeStruct((1, 1), wide)],
        out_specs=[pl.BlockSpec(memory_space=pltpu.VMEM)] * 7
        + [pl.BlockSpec(memory_space=pltpu.SMEM)],
        name="squares",
    )(own[0], own[1], spots)

    summed = everywhere_sum(jnp.stack([squares[0, 0], loss_part / (patch_count * n_mp)]))
    grad_norm = jnp.sqrt(summed[0])
    param_count = 2 * sum(
        masters[which].size * n_dp * (n_mp if which < 4 else 1) for which in range(7)
    )
    limit = clip_scale * math.sqrt(param_count / patch_count)
    factor = jnp.minimum(1.0, limit / grad_norm)
    steps_done = step_count[0].astype(wide)
    fix_one = 1.0 - beta_one**steps_done
    fix_two = 1.0 - beta_two**steps_done
    arrays = []
    for which in range(6):
        arrays.append(grads[which])
        arrays += [flat(x[which], which) for x in (masters, firsts, seconds)]
    fresh = call(
        adam_kernel,
        "adam",
        [jnp.stack([factor, fix_one, fix_two])],
        arrays,
        [(shapes[which], wide) for which in range(6) for _ in range(3)],
        near=False,
    )
    results = [summed[1], grad_norm]
    for at, x in enumerate(fresh):
        results.append((x.T if at // 3 in (3, 5) else x)[None])
    results += adam_step(
        grads[6][None], gains, gains_first, gains_second, factor, fix_one, fix_two, gain_rate, 0.0
    )
    return tuple(results)


def solution(mesh):
    split_rows = P("section", "dp", "mp")
    split_columns = P("section", "mp", "dp")
    weights = (
        split_rows,
        split_columns,
        split_rows,
        split_columns,
        P("section", "dp", None),
        P("section", None, "dp"),
        P("section", None, "dp"),
    )
    return jax.shard_map(
        local,
        mesh=mesh,
        in_specs=(P("dp", None, None), P("dp", None, None), P("dp"), P("dp"), P()) + weights * 3,
        out_specs=(P(), P()) + tuple(spec for spec in weights for _ in range(3)),
        check_vma=False,
    )
```

```python
import functools
import itertools
import math

import jax
import jax.numpy as jnp
from jax import lax
from jax.experimental import pallas as pl
from jax.experimental.pallas import tpu as pltpu
from jax.sharding import PartitionSpec as P

HEAD = 64
PDIM = 48
NCLASS = 1000
LANES = 128
GRANT = 8 << 20
GRAD_GRANT = 14 << 20

ln_eps = 1e-06
pen_weight = 0.5
noise_scale = 0.1
beta_one = 0.9
beta_two = 0.95
adam_eps = 1e-08
learn_rate = 0.05
gain_rate = 0.4
decay_rate = 0.1
clip_scale = 0.01
gelu_c = math.sqrt(2.0 / math.pi)
gelu_a = 0.044715
low = jnp.bfloat16
wide = jnp.float32
ints = jnp.int32


def dot(a, b, ca, cb):
    return lax.dot_general(a, b, (((ca,), (cb,)), ((), ())), preferred_element_type=wide)


def iota(shape, dim):
    return lax.broadcasted_iota(ints, shape, dim)


def up_to(width):
    return -(-width // LANES) * LANES


def call(body, name, scalars, arrays, outs, flops=0, trans=0, after=(), near=True, grant=GRANT):
    nbytes = sum(a.size * a.dtype.itemsize for a in arrays)
    nbytes += sum(math.prod(s) * jnp.dtype(d).itemsize for s, d in outs)
    arrays = [pltpu.with_memory_space_constraint(a, pltpu.VMEM) for a in arrays]
    count = len(scalars) + len(arrays)

    def kernel(*refs):
        body(*refs[:count], *refs[count + len(after) :])

    return pl.pallas_call(
        kernel,
        out_shape=[pltpu.VMEM(s, d) if near else jax.ShapeDtypeStruct(s, d) for s, d in outs],
        in_specs=[pl.BlockSpec(memory_space=pltpu.SMEM)] * len(scalars)
        + [pl.BlockSpec(memory_space=pltpu.VMEM)] * len(arrays)
        + [pl.BlockSpec(memory_space=pl.ANY)] * len(after),
        name=name,
        compiler_params=pltpu.CompilerParams(vmem_limit_bytes=grant),
        cost_estimate=pl.CostEstimate(flops=flops, bytes_accessed=nbytes, transcendentals=trans),
    )(*scalars, *arrays, *after)


def gate(x, tokens):
    def kernel(*refs):
        del refs

    return pl.pallas_call(
        kernel,
        out_shape=jax.ShapeDtypeStruct(x.shape, x.dtype),
        in_specs=[pl.BlockSpec(memory_space=pl.ANY)] * (1 + len(tokens)),
        out_specs=pl.BlockSpec(memory_space=pl.ANY),
        input_output_aliases={0: 0},
        name="gate",
        compiler_params=pltpu.CompilerParams(vmem_limit_bytes=1 << 20),
    )(x, *tokens)


def norm_parts(h):
    centered = h - jnp.mean(h, -1, keepdims=True)
    inv = lax.rsqrt(jnp.mean(centered * centered, -1, keepdims=True) + ln_eps)
    return centered * inv, inv


def norm_back(dout, gain, n, inv):
    dn = dout * gain
    dh = inv * (dn - jnp.mean(dn, -1, keepdims=True) - n * jnp.mean(dn * n, -1, keepdims=True))
    return dh, jnp.sum(dout * n, 0, keepdims=True)


def causal_mask(size, flip):
    query, key = iota((size, size), 0), iota((size, size), 1)
    return key >= query if flip else query >= key


def head_probs(q, k, mask):
    scores = dot(q, k, 1, 1) * (1.0 / math.sqrt(HEAD))
    scores = jnp.where(mask, scores, -1e30)
    raised = jnp.exp(scores - jnp.max(scores, -1, keepdims=True))
    return raised / jnp.sum(raised, -1, keepdims=True)


def prev_rows(x, flip):
    rows = x.shape[0]
    first = rows - 1 if flip else 0
    rolled = pltpu.roll(x, rows - 1 if flip else 1, 0)
    return jnp.where(iota(x.shape, 0) == first, 0.0, rolled)


def next_rows(x, flip):
    rows = x.shape[0]
    last = 0 if flip else rows - 1
    rolled = pltpu.roll(x, 1 if flip else rows - 1, 0)
    return jnp.where(iota(x.shape, 0) == last, 0.0, rolled)


def joined(a, a_in):
    return a[...].astype(wide) + a_in[...].astype(wide)


class Plan:
    def __init__(self, patches, n_img, classes, d_head, d_qkv, d_out):
        self.fixed = PDIM + patches
        self.gain_at = self.fixed
        self.class_at = self.fixed + 8
        self.table_w = up_to(self.class_at + n_img)
        self.head_at = self.table_w
        self.out_at = self.head_at + up_to(d_head)
        self.qkv_at = self.out_at + up_to(d_out)
        self.qkv = d_qkv
        self.width = self.qkv_at + up_to(d_qkv)
        self.d_head = d_head
        self.d_out = d_out


def enter_kernel(plan, flip, img, f, pw, gains, left, h0, a1, qkv, ctx, part):
    rows = f.shape[0]
    at, row = iota((rows, plan.table_w), 1), iota((rows, plan.table_w), 0)
    spot = (rows - 1 - row if flip else row) + PDIM
    picked = (at == spot) | (at == plan.class_at + img[0])
    base = picked.astype(wide)
    first = jnp.where(iota((rows, LANES), 1) < PDIM, f[...], base[:, :LANES])
    left[:, :LANES] = first.astype(low)
    left[:, LANES:] = base[:, LANES:].astype(low)
    h = dot(left[...], pw[:, : plan.table_w], 1, 1)
    h0[...] = h
    n, _ = norm_parts(h)
    a = (n * gains[0:1]).astype(low)
    a1[...] = a
    qkv[...] = dot(a, pw[:, plan.qkv_at : plan.qkv_at + plan.qkv], 1, 0).astype(low)
    mask = causal_mask(rows, flip)
    for k in range(plan.d_out // HEAD):
        at = k * 3 * HEAD
        q, key, v = (qkv[:, at + j * HEAD : at + (j + 1) * HEAD] for j in range(3))
        probs = head_probs(q, key, mask)
        ctx[:, k * HEAD : (k + 1) * HEAD] = dot(probs.astype(low), v, 1, 0).astype(low)
    part[...] = dot(ctx[...], pw[:, plan.out_at : plan.out_at + plan.d_out], 1, 1).astype(low)


def ff_kernel(h0, a, a_in, fw, gains, h1, a2, upper, hidden, part):
    hid = upper.shape[1]
    h = h0[...] + joined(a, a_in)
    h1[...] = h
    n, _ = norm_parts(h)
    x = (n * gains[1:2]).astype(low)
    a2[...] = x
    u = dot(x, fw[:, :hid], 1, 0)
    upper[...] = u
    act = (0.5 * u * (1.0 + jnp.tanh(gelu_c * (u + gelu_a * u * u * u)))).astype(low)
    hidden[...] = act
    part[...] = dot(act, fw[:, hid:], 1, 1).astype(low)


def head_kernel(plan, flip, h1, a, a_in, f, pw, gains, h2, a3, scale, z, sums):
    rows = f.shape[0]
    h = h1[...] + joined(a, a_in)
    h2[...] = h
    n, _ = norm_parts(h)
    x = (n * gains[2:3]).astype(low)
    a3[...] = x
    y = dot(x, pw[:, plan.head_at : plan.head_at + LANES], 1, 0)
    here = iota(y.shape, 1) < PDIM
    shift = jnp.where(here, y, 0.0)
    sc = jnp.where(here, pltpu.roll(y, LANES - PDIM, 1), 0.0)
    scale[...] = sc
    out = (f[...] - prev_rows(shift, flip)) * jnp.exp(-prev_rows(sc, flip))
    z[...] = out
    used = iota(y.shape, 0) != (0 if flip else rows - 1)
    term = jnp.where(used, sc + pen_weight * sc * sc, 0.0)
    sums[0:1] = jnp.sum(term, 0, keepdims=True)
    sums[1:2] = jnp.sum(out * out, 0, keepdims=True)


def head_back_kernel(plan, flip, last, patch_count, *refs):
    if not last:
        gz_ref, *refs = refs
    z, scale, h2, upper, pw, fw, gains, df, dy, dh2, dh2_low, dupper, part, dg = refs
    hid = upper.shape[1]
    rows = z.shape[0]
    gz = z[...] / patch_count if last else gz_ref[...]
    sc = scale[...]
    d = gz * jnp.exp(-prev_rows(sc, flip))
    df[...] = d
    here = iota(sc.shape, 1) < PDIM
    used = (iota(sc.shape, 0) != (0 if flip else rows - 1)) & here
    inner = jnp.where(used, (1.0 + 2.0 * pen_weight * sc) / patch_count, 0.0)
    dscale = inner + next_rows(-gz * z[...], flip)
    dshift = next_rows(-d, flip)
    at = iota(sc.shape, 1)
    dout = jnp.where(here, dshift, pltpu.roll(dscale, PDIM, 1))
    dout = jnp.where(at < 2 * PDIM, dout, 0.0).astype(low)
    dy[...] = dout
    n, inv = norm_parts(h2[...])
    da3 = dot(dout, pw[:, plan.head_at : plan.head_at + LANES], 1, 1)
    dh, dgain = norm_back(da3, gains[2:3], n, inv)
    dg[...] = dgain
    dh2[...] = dh
    dh_low = dh.astype(low)
    dh2_low[...] = dh_low
    dhidden = dot(dh_low, fw[:, hid:], 1, 0)
    u = upper[...]
    t = jnp.tanh(gelu_c * (u + gelu_a * u * u * u))
    slope = 0.5 * (1.0 + t) + 0.5 * u * (1.0 - t * t) * gelu_c * (1.0 + 3.0 * gelu_a * u * u)
    du = (dhidden * slope).astype(low)
    dupper[...] = du
    part[...] = dot(du, fw[:, :hid], 1, 1).astype(low)


def attend_back_kernel(
    plan, flip, dh2, a, a_in, h1, qkv, pw, gains, dh1, dh1_low, dqkv, part, dg
):
    rows = dh2.shape[0]
    n, inv = norm_parts(h1[...])
    dh, dgain = norm_back(joined(a, a_in), gains[1:2], n, inv)
    dg[...] = dgain
    total = dh2[...] + dh
    dh1[...] = total
    t_low = total.astype(low)
    dh1_low[...] = t_low
    dctx_all = dot(t_low, pw[:, plan.out_at : plan.out_at + plan.d_out], 1, 0).astype(low)
    mask = causal_mask(rows, flip)
    inv_root = 1.0 / math.sqrt(HEAD)
    for k in range(plan.d_out // HEAD):
        at = k * 3 * HEAD
        q, key, v = (qkv[:, at + j * HEAD : at + (j + 1) * HEAD] for j in range(3))
        dctx = dctx_all[:, k * HEAD : (k + 1) * HEAD]
        probs = head_probs(q, key, mask)
        dprobs = dot(dctx, v, 1, 1)
        dscores = (probs * (dprobs - jnp.sum(dprobs * probs, -1, keepdims=True))).astype(low)
        dqkv[:, at : at + HEAD] = (dot(dscores, key, 1, 0) * inv_root).astype(low)
        dqkv[:, at + HEAD : at + 2 * HEAD] = (dot(dscores, q, 0, 0) * inv_root).astype(low)
        dqkv[:, at + 2 * HEAD : at + 3 * HEAD] = dot(probs.astype(low), dctx, 0, 0).astype(low)
    part[...] = dot(dqkv[...], pw[:, plan.qkv_at : plan.qkv_at + plan.qkv], 1, 1).astype(low)


def leave_back_kernel(plan, through, dh1, a, a_in, h0, gains, *refs):
    n, inv = norm_parts(h0[...])
    dh, dgain = norm_back(joined(a, a_in), gains[0:1], n, inv)
    if through:
        df, pw, dh0_low, dg, gz = refs
    else:
        dh0_low, dg = refs
    dg[...] = dgain
    total = (dh1[...] + dh).astype(low)
    dh0_low[...] = total
    if through:
        back = dot(total, pw[:, :LANES], 1, 0)
        gz[...] = df[...] + jnp.where(iota(back.shape, 1) < PDIM, back, 0.0)


def place(value, keep, send, start):
    half, columns = value.shape[0] // 2, slice(start, start + value.shape[1])
    keep[:, columns] = value[:half]
    send[:, columns] = value[half:]


def ff_grad_kernel(count, *refs):
    a2, dupper, dh2, hidden = (refs[j * count : (j + 1) * count] for j in range(4))
    keep, send = refs[4 * count :]
    up = sum(dot(x[...], y[...], 0, 0) for x, y in zip(a2, dupper)).astype(low)
    place(up, keep, send, 0)
    down = sum(dot(x[...], y[...], 0, 0) for x, y in zip(dh2, hidden)).astype(low)
    place(down, keep, send, up.shape[1])


def attend_grad_kernel(plan, count, *refs):
    a1, dqkv, dh1, ctx, dh0, left, a3, dy = (refs[j * count : (j + 1) * count] for j in range(8))
    dgains, keep, send = refs[8 * count :]
    qkv = sum(dot(x[...], y[...], 0, 0) for x, y in zip(a1, dqkv)).astype(low)
    qkv = jnp.pad(qkv, ((0, 0), (0, plan.width - plan.qkv_at - plan.qkv)))
    place(qkv, keep, send, plan.qkv_at)
    out = sum(dot(x[...], y[...], 0, 0) for x, y in zip(dh1, ctx)).astype(low)
    out = jnp.pad(out, ((0, 0), (0, plan.qkv_at - plan.out_at - plan.d_out)))
    place(out, keep, send, plan.out_at)
    head = sum(dot(x[...], y[...], 0, 0) for x, y in zip(a3, dy)).astype(low)
    place(head, keep, send, plan.head_at)
    table = sum(dot(x[...], y[...], 0, 0) for x, y in zip(dh0, left))
    shape = (8, plan.table_w)
    spot = (iota(shape, 1) == plan.gain_at + iota(shape, 0)).astype(low)
    table = table + dot(dgains[...].astype(low), spot, 0, 0)
    place(table.astype(low), keep, send, 0)


def join_kernel(one, two, out):
    half = one.shape[0]
    out[:half] = one[...]
    out[half:] = two[...]


def square_kernel(plan, n_mp, gp, fp, spots, qkv, out, up, down, head, table, gains, sq):
    hid = up.shape[1]
    g = gp[:, plan.qkv_at : plan.qkv_at + plan.qkv].astype(wide)
    qkv[...] = g
    total = jnp.sum(g * g)
    turn = (iota((plan.d_out, plan.d_out), 0) == iota((plan.d_out, plan.d_out), 1)).astype(low)
    g = dot(turn, gp[:, plan.out_at : plan.out_at + plan.d_out], 1, 1)
    out[...] = g
    total = total + jnp.sum(g * g)
    for source, target in ((fp[:, :hid], up), (fp[:, hid:], down)):
        g = source.astype(wide)
        target[...] = g
        total = total + jnp.sum(g * g)
    g = gp[:, plan.head_at : plan.head_at + plan.d_head].astype(wide)
    head[...] = g
    copied = jnp.sum(g * g)
    packed = gp[:, : plan.table_w]
    width = table.shape[1]
    pick = (spots[...] == iota((plan.table_w, width), 1)).astype(low)
    g = dot(packed, pick, 1, 0)
    table[...] = g
    copied = copied + jnp.sum(g * g)
    shape = (8, plan.table_w)
    spot = (iota(shape, 1) == plan.gain_at + iota(shape, 0)) & (iota(shape, 0) < 3)
    g = dot(spot.astype(low), packed, 1, 1)
    gains[...] = g[:3]
    copied = copied + jnp.sum(g * g)
    sq[0, 0] = total + copied / n_mp


def adam_step(g, w, m, v, factor, fix_one, fix_two, rate, decay):
    clipped = g * factor
    first = beta_one * m + (1.0 - beta_one) * clipped
    second = beta_two * v + (1.0 - beta_two) * clipped * clipped
    step = first / fix_one / (jnp.sqrt(second / fix_two) + adam_eps)
    return w - rate * (step + decay * w), first, second


def adam_kernel(scalars, *refs):
    factor, fix_one, fix_two = scalars[0], scalars[1], scalars[2]
    ins, outs = refs[:24], refs[24:]
    for which in range(6):
        g, w, m, v = ins[4 * which : 4 * which + 4]
        w_out, m_out, v_out = outs[3 * which : 3 * which + 3]
        values = (g[...], w[...], m[...], v[...])
        w_out[...], m_out[...], v_out[...] = adam_step(
            *values, factor, fix_one, fix_two, learn_rate, decay_rate
        )


def swap(x, axis, bit):
    return lax.ppermute(x, axis, [(j, j ^ bit) for j in range(lax.axis_size(axis))])


def swap_cores(x):
    return swap(x, "section", 1)


def mp_sum(part, turn):
    if lax.axis_size("mp") != 4:
        part = lax.psum(part, "mp")
        return part, jnp.zeros_like(part)
    bits = (1, 2) if turn % 2 == 0 else (2, 1)
    part = (part.astype(wide) + swap(part, "mp", bits[0]).astype(wide)).astype(low)
    return part, swap(part, "mp", bits[1])


def slots(x, axis):
    size = lax.axis_size(axis)
    if size > 4:
        return lax.all_gather(x, axis, axis=0)
    mine = lax.dynamic_update_slice_in_dim(
        jnp.zeros((size,) + x.shape, x.dtype), x[None], lax.axis_index(axis), 0
    )
    total = mine
    for by in range(1, size):
        total = total + lax.ppermute(mine, axis, [(j, (j + by) % size) for j in range(size)])
    return total


def everywhere_sum(vector):
    for axis in ("section", "mp", "dp"):
        vector = jnp.sum(slots(vector, axis), 0)
    return vector


def pad_columns(x, width):
    return jnp.pad(x, ((0, 0), (0, width - x.shape[1])))


def local(
    images,
    noise,
    labels,
    drop_mask,
    step_count,
    qkv_weight,
    attn_out_weight,
    up_weight,
    down_weight,
    head_weight,
    embed_table,
    gains,
    qkv_first,
    attn_out_first,
    up_first,
    down_first,
    head_first,
    embed_first,
    gains_first,
    qkv_second,
    attn_out_second,
    up_second,
    down_second,
    head_second,
    embed_second,
    gains_second,
):
    masters = (qkv_weight, attn_out_weight, up_weight, down_weight, head_weight, embed_table, gains)
    firsts = (qkv_first, attn_out_first, up_first, down_first, head_first, embed_first, gains_first)
    seconds = (
        qkv_second,
        attn_out_second,
        up_second,
        down_second,
        head_second,
        embed_second,
        gains_second,
    )
    section = lax.axis_index("section")
    n_dp = lax.axis_size("dp")
    n_mp = lax.axis_size("mp")
    here, patches = images.shape[0], images.shape[1]
    mine = here // 2
    n_img = here * n_dp
    patch_count = n_img * patches
    fixed = PDIM + patches
    classes = embed_table.shape[1] - fixed
    model = embed_table.shape[2] * n_dp
    hid = up_weight.shape[2]
    plan = Plan(
        patches,
        n_img,
        classes,
        head_weight.shape[2],
        qkv_weight.shape[2],
        attn_out_weight.shape[1],
    )

    tags = slots(jnp.where(drop_mask == 1, NCLASS, labels), "dp").reshape(n_img)
    table_t = embed_table[0].T.astype(low)
    ids = fixed + tags
    hot = (ids[:, None] == iota((n_img, fixed + classes), 1)).astype(low)
    class_t = dot(table_t, hot, 1, 1).astype(low)
    gains_t = pad_columns(gains[0].T.astype(low), 8)
    packets = (
        jnp.concatenate(
            [
                pad_columns(
                    jnp.concatenate([table_t[:, :fixed], gains_t, class_t], 1), plan.table_w
                ),
                pad_columns(head_weight[0].astype(low), plan.out_at - plan.head_at),
                pad_columns(attn_out_weight[0].T.astype(low), plan.qkv_at - plan.out_at),
                pad_columns(qkv_weight[0].astype(low), plan.width - plan.qkv_at),
            ],
            1,
        ),
        jnp.concatenate([up_weight[0].astype(low), down_weight[0].T.astype(low)], 1),
    )

    def spread(packet):
        rows = packet.shape[0] // 2
        low_rows, high_rows = packet[:rows], packet[rows:]
        moved = swap_cores(jnp.where(section == 0, high_rows, low_rows))
        return jnp.where(section == 0, low_rows, moved), jnp.where(section == 0, moved, high_rows)

    spread_packets = [spread(packet) for packet in packets]

    def gather(packet, block, tokens=()):
        own_rows = lax.all_gather(spread_packets[packet][block], "dp", axis=0, tiled=True)
        if tokens:
            own_rows = gate(own_rows, tokens)
        other = swap_cores(own_rows)
        rows, width = own_rows.shape
        return call(join_kernel, "join", [], [own_rows, other], [((2 * rows, width), low)])[0]

    def gain_rows(pw):
        shape = (8, plan.table_w)
        spot = (iota(shape, 1) == plan.gain_at + iota(shape, 0)) & (iota(shape, 0) < 3)
        return dot(spot.astype(low), pw[:, : plan.table_w], 1, 1)

    def own_images(x):
        return lax.dynamic_slice_in_dim(x, section * mine, mine, 0)

    inputs = own_images(images) + noise_scale * own_images(noise)
    inputs = jnp.pad(inputs, ((0, 0), (0, 0), (0, LANES - PDIM)))
    latents = [inputs[k] for k in range(mine)]
    first_image = lax.axis_index("dp") * here + section * mine
    full = (patches, model)
    tile = (patches, LANES)
    mac = 2 * patches * model
    loss_part = 0.0
    kept = []
    turns = itertools.count()

    def exchange(part):
        return mp_sum(part, next(turns))

    def sent(saved):
        return [s["p"][1] for s in saved[:-1]] + [saved[-1]["p"][0]]

    weights = []
    for block in range(2):
        pw = gather(0, block, sent(kept[0]) if block else ())
        rows = gain_rows(pw)
        flip = block == 1
        saved = []
        before = []
        for k in range(mine):
            left, h0, a1, qkv, ctx, part = call(
                functools.partial(enter_kernel, plan, flip),
                "enter",
                [(first_image + k)[None].astype(ints)],
                [latents[k], pw, rows],
                [
                    ((patches, plan.table_w), low),
                    (full, wide),
                    (full, low),
                    ((patches, plan.qkv), low),
                    ((patches, plan.d_out), low),
                    (full, low),
                ],
                mac * (plan.table_w + plan.qkv + plan.d_out),
                patches * patches * 4,
                after=before,
            )
            before = [part]
            saved.append(
                dict(f=latents[k], left=left, h0=h0, a1=a1, qkv=qkv, ctx=ctx, p=exchange(part))
            )
        fw = gather(1, block, sent(saved))
        weights.append((pw, fw, rows))
        for k, kept_k in enumerate(saved):
            h1, a2, upper, hidden, part = call(
                ff_kernel,
                "ff",
                [],
                [kept_k["h0"], *kept_k["p"], fw, rows],
                [
                    (full, wide),
                    (full, low),
                    ((patches, hid), wide),
                    ((patches, hid), low),
                    (full, low),
                ],
                mac * hid * 2,
                patches * hid,
                after=before,
            )
            before = [part]
            kept_k.update(h1=h1, a2=a2, upper=upper, hidden=hidden, p=exchange(part))
        for kept_k in saved:
            h2, a3, scale, z, sums = call(
                functools.partial(head_kernel, plan, flip),
                "head",
                [],
                [kept_k["h1"], *kept_k["p"], kept_k["f"], pw, rows],
                [(full, wide), (full, low), (tile, wide), (tile, wide), ((2, LANES), wide)],
                mac * LANES,
                patches * LANES,
            )
            kept_k.update(h2=h2, a3=a3, scale=scale, z=z)
            loss_part = loss_part + jnp.sum(sums[0])
            if block == 1:
                loss_part = loss_part + 0.5 * jnp.sum(sums[1])
        latents = [kept_k["z"] for kept_k in saved]
        kept.append(saved)

    grads_z = [None] * mine
    scattered = [None, None]

    def scatter(pair):
        keep, send = pair
        other = swap_cores(send)
        both = (keep.astype(wide) + other.astype(wide)).astype(low)
        return both, lax.psum_scatter(both, "dp", scatter_dimension=0, tiled=True)

    pending = []

    for block in (1, 0):
        pw, fw, rows = weights[block]
        flip = block == 1
        saved = kept[block]
        before = []
        for k in range(mine):
            s = saved[k]
            df, dy, dh2, dh2_low, dupper, part, dg2 = call(
                functools.partial(head_back_kernel, plan, flip, block == 1, float(patch_count)),
                "head_back",
                [],
                ([] if block == 1 else [grads_z[k]])
                + [s["z"], s["scale"], s["h2"], s["upper"], pw, fw, rows],
                [
                    (tile, wide),
                    (tile, low),
                    (full, wide),
                    (full, low),
                    ((patches, hid), low),
                    (full, low),
                    ((1, model), wide),
                ],
                mac * (LANES + 2 * hid),
                patches * hid,
                after=before,
            )
            before = [part]
            s.update(
                df=df, dy=dy, dh2=dh2, dh2_low=dh2_low, dupper=dupper, dg2=dg2, p=exchange(part)
            )
        ff_grads = call(
            functools.partial(ff_grad_kernel, mine),
            "ff_grad",
            [],
            [s[name] for name in ("a2", "dupper", "dh2_low", "hidden") for s in saved],
            [((model // 2, 2 * hid), low)] * 2,
            mac * hid * 2 * mine,
            after=[] if block else [attend_grads[0]],
            grant=GRAD_GRANT,
        )
        before = before + [ff_grads[0]]
        summed_ff, ff_scattered = scatter(ff_grads)
        pending.append(summed_ff)
        for k in range(mine):
            s = saved[k]
            dh1, dh1_low, dqkv, part, dg1 = call(
                functools.partial(attend_back_kernel, plan, flip),
                "attend_back",
                [],
                [s["dh2"], *s["p"], s["h1"], s["qkv"], pw, rows],
                [
                    (full, wide),
                    (full, low),
                    ((patches, plan.qkv), low),
                    (full, low),
                    ((1, model), wide),
                ],
                mac * (plan.d_out * 2 + plan.qkv),
                patches * patches * 4,
                after=before + (pending if k == 1 else []),
            )
            before = [part]
            s.update(dh1=dh1, dh1_low=dh1_low, dqkv=dqkv, dg1=dg1, p=exchange(part))
        for k in range(mine):
            s = saved[k]
            outs = call(
                functools.partial(leave_back_kernel, plan, block == 1),
                "leave_back",
                [],
                [s["dh1"], *s["p"], s["h0"], rows] + ([s["df"], pw] if block == 1 else []),
                [(full, low), ((1, model), wide)] + ([(tile, wide)] if block == 1 else []),
                mac * LANES,
            )
            s.update(dh0=outs[0], dg0=outs[1])
            if block == 1:
                grads_z[k] = outs[2]
        dgains = jnp.concatenate(
            [sum(s[name] for s in saved) for name in ("dg0", "dg1", "dg2")]
            + [jnp.zeros((5, model), wide)],
            0,
        )
        names = ("a1", "dqkv", "dh1_low", "ctx", "dh0", "left", "a3", "dy")
        attend_grads = call(
            functools.partial(attend_grad_kernel, plan, mine),
            "attend_grad",
            [],
            [s[name] for name in names for s in saved] + [dgains],
            [((model // 2, plan.width), low)] * 2,
            mac * plan.width * mine,
            grant=GRAD_GRANT,
        )
        summed_attend, attend_scattered = scatter(attend_grads)
        pending = [summed_attend]
        scattered[block] = (attend_scattered, ff_scattered)

    own = []
    for at in range(2):
        zero, one = scattered[0][at], scattered[1][at]
        moved = swap_cores(jnp.where(section == 0, one, zero))
        own.append(
            jnp.where(
                section == 0,
                jnp.concatenate([zero, moved], 0),
                jnp.concatenate([moved, one], 0),
            )
        )

    spots = jnp.concatenate(
        [
            jnp.arange(fixed, dtype=ints),
            jnp.full((8,), -1, ints),
            ids.astype(ints),
            jnp.full((plan.table_w - plan.class_at - n_img,), -1, ints),
        ]
    )[:, None]

    def flat(x, which):
        return x[0].T if which in (3, 5) else x[0]

    shapes = [flat(w, which).shape for which, w in enumerate(masters)]
    *grads, squares = pl.pallas_call(
        functools.partial(square_kernel, plan, float(n_mp)),
        out_shape=[pltpu.VMEM(s, wide) for s in shapes]
        + [jax.ShapeDtypeStruct((1, 1), wide)],
        out_specs=[pl.BlockSpec(memory_space=pltpu.VMEM)] * 7
        + [pl.BlockSpec(memory_space=pltpu.SMEM)],
        name="squares",
        compiler_params=pltpu.CompilerParams(vmem_limit_bytes=GRAD_GRANT),
    )(*(pltpu.with_memory_space_constraint(x, pltpu.VMEM) for x in (*own, spots)))

    summed = everywhere_sum(jnp.stack([squares[0, 0], loss_part / (patch_count * n_mp)]))
    grad_norm = jnp.sqrt(summed[0])
    param_count = 2 * sum(
        masters[which].size * n_dp * (n_mp if which < 4 else 1) for which in range(7)
    )
    limit = clip_scale * math.sqrt(param_count / patch_count)
    factor = jnp.minimum(1.0, limit / grad_norm)
    steps_done = step_count[0].astype(wide)
    fix_one = 1.0 - beta_one**steps_done
    fix_two = 1.0 - beta_two**steps_done
    arrays = []
    for which in range(6):
        arrays.append(grads[which])
        arrays += [flat(x[which], which) for x in (masters, firsts, seconds)]
    fresh = call(
        adam_kernel,
        "adam",
        [jnp.stack([factor, fix_one, fix_two])],
        arrays,
        [(shapes[which], wide) for which in range(6) for _ in range(3)],
        near=False,
        grant=GRAD_GRANT,
    )
    results = [summed[1], grad_norm]
    for at, x in enumerate(fresh):
        results.append((x.T if at // 3 in (3, 5) else x)[None])
    results += adam_step(
        grads[6][None], gains, gains_first, gains_second, factor, fix_one, fix_two, gain_rate, 0.0
    )
    return tuple(results)


def solution(mesh):
    split_rows = P("section", "dp", "mp")
    split_columns = P("section", "mp", "dp")
    weights = (
        split_rows,
        split_columns,
        split_rows,
        split_columns,
        P("section", "dp", None),
        P("section", None, "dp"),
        P("section", None, "dp"),
    )
    return jax.shard_map(
        local,
        mesh=mesh,
        in_specs=(P("dp", None, None), P("dp", None, None), P("dp"), P("dp"), P()) + weights * 3,
        out_specs=(P(), P()) + tuple(spec for spec in weights for _ in range(3)),
        check_vma=False,
    )
```

```python
import functools
import itertools
import math

import jax
import jax.numpy as jnp
from jax import lax
from jax.experimental import pallas as pl
from jax.experimental.pallas import tpu as pltpu
from jax.sharding import PartitionSpec as P

HEAD = 64
PDIM = 48
NCLASS = 1000
LANES = 128
GRANT = 6 << 20
LARGE_GRANT = 12 << 20

ln_eps = 1e-06
pen_weight = 0.5
noise_scale = 0.1
beta_one = 0.9
beta_two = 0.95
adam_eps = 1e-08
learn_rate = 0.05
gain_rate = 0.4
decay_rate = 0.1
clip_scale = 0.01
gelu_c = math.sqrt(2.0 / math.pi)
gelu_a = 0.044715
low = jnp.bfloat16
wide = jnp.float32
ints = jnp.int32


def dot(a, b, ca, cb):
    return lax.dot_general(a, b, (((ca,), (cb,)), ((), ())), preferred_element_type=wide)


def iota(shape, dim):
    return lax.broadcasted_iota(ints, shape, dim)


def up_to(width):
    return -(-width // LANES) * LANES


def near(x):
    return pltpu.with_memory_space_constraint(x, pltpu.VMEM)


def call(body, name, scalars, arrays, outs, flops=0, trans=0, after=(), grant=GRANT):
    nbytes = sum(a.size * a.dtype.itemsize for a in arrays)
    nbytes += sum(math.prod(s) * jnp.dtype(d).itemsize for s, d, _ in outs)
    count = len(scalars) + len(arrays)

    def kernel(*refs):
        body(*refs[:count], *refs[count + len(after) :])

    return pl.pallas_call(
        kernel,
        out_shape=[pltpu.VMEM(s, d) if n else pltpu.HBM(s, d) for s, d, n in outs],
        out_specs=[pl.BlockSpec(memory_space=pltpu.VMEM)] * len(outs),
        in_specs=[pl.BlockSpec(memory_space=pltpu.SMEM)] * len(scalars)
        + [pl.BlockSpec(memory_space=pltpu.VMEM)] * len(arrays)
        + [pl.BlockSpec(memory_space=pl.ANY)] * len(after),
        name=name,
        compiler_params=pltpu.CompilerParams(vmem_limit_bytes=grant),
        cost_estimate=pl.CostEstimate(flops=flops, bytes_accessed=nbytes, transcendentals=trans),
    )(*scalars, *arrays, *after)


def gate(x, tokens):
    def kernel(*refs):
        del refs

    return pl.pallas_call(
        kernel,
        out_shape=jax.ShapeDtypeStruct(x.shape, x.dtype),
        in_specs=[pl.BlockSpec(memory_space=pl.ANY)] * (1 + len(tokens)),
        out_specs=pl.BlockSpec(memory_space=pl.ANY),
        input_output_aliases={0: 0},
        name="gate",
        compiler_params=pltpu.CompilerParams(vmem_limit_bytes=1 << 20),
    )(x, *tokens)


def norm_parts(h):
    centered = h - jnp.mean(h, -1, keepdims=True)
    inv = lax.rsqrt(jnp.mean(centered * centered, -1, keepdims=True) + ln_eps)
    return centered * inv, inv


def norm_back(dout, gain, n, inv):
    dn = dout * gain
    dh = inv * (dn - jnp.mean(dn, -1, keepdims=True) - n * jnp.mean(dn * n, -1, keepdims=True))
    return dh, jnp.sum(dout * n, 0, keepdims=True)


def causal_mask(size, flip):
    query, key = iota((size, size), 0), iota((size, size), 1)
    return key >= query if flip else query >= key


def head_probs(q, k, mask):
    scores = dot(q, k, 1, 1) * (1.0 / math.sqrt(HEAD))
    scores = jnp.where(mask, scores, -1e30)
    raised = jnp.exp(scores - jnp.max(scores, -1, keepdims=True))
    return raised / jnp.sum(raised, -1, keepdims=True)


def prev_rows(x, flip):
    rows = x.shape[0]
    first = rows - 1 if flip else 0
    rolled = pltpu.roll(x, rows - 1 if flip else 1, 0)
    return jnp.where(iota(x.shape, 0) == first, 0.0, rolled)


def next_rows(x, flip):
    rows = x.shape[0]
    last = 0 if flip else rows - 1
    rolled = pltpu.roll(x, 1 if flip else rows - 1, 0)
    return jnp.where(iota(x.shape, 0) == last, 0.0, rolled)


def joined(a, a_in):
    return a[...].astype(wide) + a_in[...].astype(wide)


class Plan:
    def __init__(self, patches, n_img, classes, d_head, d_qkv, d_out):
        self.fixed = PDIM + patches
        self.gain_at = self.fixed
        self.class_at = self.fixed + 8
        self.table_w = up_to(self.class_at + n_img)
        self.head_at = self.table_w
        self.out_at = self.head_at + up_to(d_head)
        self.qkv_at = self.out_at + up_to(d_out)
        self.qkv = d_qkv
        self.width = self.qkv_at + up_to(d_qkv)
        self.d_head = d_head
        self.d_out = d_out


def left_operand(plan, flip, f, image):
    rows = f.shape[0]
    at, row = iota((rows, plan.table_w), 1), iota((rows, plan.table_w), 0)
    spot = (rows - 1 - row if flip else row) + PDIM
    base = ((at == spot) | (at == plan.class_at + image)).astype(wide)
    first = jnp.where(iota((rows, LANES), 1) < PDIM, f, base[:, :LANES])
    return jnp.concatenate([first.astype(low), base[:, LANES:].astype(low)], 1)


def enter_kernel(plan, flip, img, f, pw, gains, h0, qkv, part):
    rows = f.shape[0]
    h = dot(left_operand(plan, flip, f[...], img[0]), pw[:, : plan.table_w], 1, 1)
    h0[...] = h
    n, _ = norm_parts(h)
    a = (n * gains[0:1]).astype(low)
    qkv[...] = dot(a, pw[:, plan.qkv_at : plan.qkv_at + plan.qkv], 1, 0).astype(low)
    mask = causal_mask(rows, flip)
    heads = []
    for k in range(plan.d_out // HEAD):
        at = k * 3 * HEAD
        q, key, v = (qkv[:, at + j * HEAD : at + (j + 1) * HEAD] for j in range(3))
        heads.append(dot(head_probs(q, key, mask).astype(low), v, 1, 0).astype(low))
    ctx = jnp.concatenate(heads, 1)
    part[...] = dot(ctx, pw[:, plan.out_at : plan.out_at + plan.d_out], 1, 1).astype(low)


def ff_kernel(h0, a, a_in, fw, gains, h1, a2, upper, part):
    hid = upper.shape[1]
    h = h0[...] + joined(a, a_in)
    h1[...] = h
    n, _ = norm_parts(h)
    x = (n * gains[1:2]).astype(low)
    a2[...] = x
    u = dot(x, fw[:, :hid], 1, 0)
    upper[...] = u
    act = (0.5 * u * (1.0 + jnp.tanh(gelu_c * (u + gelu_a * u * u * u)))).astype(low)
    part[...] = dot(act, fw[:, hid:], 1, 1).astype(low)


def head_kernel(plan, flip, h1, a, a_in, f, pw, gains, h2, scale, z, sums):
    rows = f.shape[0]
    h = h1[...] + joined(a, a_in)
    h2[...] = h
    n, _ = norm_parts(h)
    x = (n * gains[2:3]).astype(low)
    y = dot(x, pw[:, plan.head_at : plan.head_at + LANES], 1, 0)
    here = iota(y.shape, 1) < PDIM
    shift = jnp.where(here, y, 0.0)
    sc = jnp.where(here, pltpu.roll(y, LANES - PDIM, 1), 0.0)
    scale[...] = sc
    out = (f[...] - prev_rows(shift, flip)) * jnp.exp(-prev_rows(sc, flip))
    z[...] = out
    used = iota(y.shape, 0) != (0 if flip else rows - 1)
    term = jnp.where(used, sc + pen_weight * sc * sc, 0.0)
    sums[0:1] = jnp.sum(term, 0, keepdims=True)
    sums[1:2] = jnp.sum(out * out, 0, keepdims=True)


def head_back_kernel(plan, flip, last, patch_count, *refs):
    if not last:
        gz_ref, *refs = refs
    z, scale, h2, upper, pw, fw, gains, *refs = refs
    df, dy, a3, hidden, dh2, dh2_low, dupper, part, dg = refs
    hid = upper.shape[1]
    rows = z.shape[0]
    gz = z[...] / patch_count if last else gz_ref[...]
    sc = scale[...]
    d = gz * jnp.exp(-prev_rows(sc, flip))
    df[...] = d
    here = iota(sc.shape, 1) < PDIM
    used = (iota(sc.shape, 0) != (0 if flip else rows - 1)) & here
    inner = jnp.where(used, (1.0 + 2.0 * pen_weight * sc) / patch_count, 0.0)
    dscale = inner + next_rows(-gz * z[...], flip)
    dshift = next_rows(-d, flip)
    at = iota(sc.shape, 1)
    dout = jnp.where(here, dshift, pltpu.roll(dscale, PDIM, 1))
    dout = jnp.where(at < 2 * PDIM, dout, 0.0).astype(low)
    dy[...] = dout
    n, inv = norm_parts(h2[...])
    a3[...] = (n * gains[2:3]).astype(low)
    da3 = dot(dout, pw[:, plan.head_at : plan.head_at + LANES], 1, 1)
    dh, dgain = norm_back(da3, gains[2:3], n, inv)
    dg[...] = dgain
    dh2[...] = dh
    dh_low = dh.astype(low)
    dh2_low[...] = dh_low
    dhidden = dot(dh_low, fw[:, hid:], 1, 0)
    u = upper[...]
    t = jnp.tanh(gelu_c * (u + gelu_a * u * u * u))
    hidden[...] = (0.5 * u * (1.0 + t)).astype(low)
    slope = 0.5 * (1.0 + t) + 0.5 * u * (1.0 - t * t) * gelu_c * (1.0 + 3.0 * gelu_a * u * u)
    du = (dhidden * slope).astype(low)
    dupper[...] = du
    part[...] = dot(du, fw[:, :hid], 1, 1).astype(low)


def attend_back_kernel(
    plan, flip, dh2, a, a_in, h1, h0, qkv, pw, gains, dh1, dh1_low, a1, ctx, dqkv, part, dg
):
    rows = dh2.shape[0]
    n, inv = norm_parts(h1[...])
    dh, dgain = norm_back(joined(a, a_in), gains[1:2], n, inv)
    dg[...] = dgain
    total = dh2[...] + dh
    dh1[...] = total
    a1[...] = (norm_parts(h0[...])[0] * gains[0:1]).astype(low)
    t_low = total.astype(low)
    dh1_low[...] = t_low
    dctx_all = dot(t_low, pw[:, plan.out_at : plan.out_at + plan.d_out], 1, 0).astype(low)
    mask = causal_mask(rows, flip)
    inv_root = 1.0 / math.sqrt(HEAD)
    for k in range(plan.d_out // HEAD):
        at = k * 3 * HEAD
        q, key, v = (qkv[:, at + j * HEAD : at + (j + 1) * HEAD] for j in range(3))
        dctx = dctx_all[:, k * HEAD : (k + 1) * HEAD]
        probs = head_probs(q, key, mask)
        dprobs = dot(dctx, v, 1, 1)
        ctx[:, k * HEAD : (k + 1) * HEAD] = dot(probs.astype(low), v, 1, 0).astype(low)
        dscores = (probs * (dprobs - jnp.sum(dprobs * probs, -1, keepdims=True))).astype(low)
        dqkv[:, at : at + HEAD] = (dot(dscores, key, 1, 0) * inv_root).astype(low)
        dqkv[:, at + HEAD : at + 2 * HEAD] = (dot(dscores, q, 0, 0) * inv_root).astype(low)
        dqkv[:, at + 2 * HEAD : at + 3 * HEAD] = dot(probs.astype(low), dctx, 0, 0).astype(low)
    part[...] = dot(dqkv[...], pw[:, plan.qkv_at : plan.qkv_at + plan.qkv], 1, 1).astype(low)


def leave_back_kernel(plan, through, dh1, a, a_in, h0, gains, *refs):
    n, inv = norm_parts(h0[...])
    dh, dgain = norm_back(joined(a, a_in), gains[0:1], n, inv)
    if through:
        df, pw, dh0_low, dg, gz = refs
    else:
        dh0_low, dg = refs
    dg[...] = dgain
    total = (dh1[...] + dh).astype(low)
    dh0_low[...] = total
    if through:
        back = dot(total, pw[:, :LANES], 1, 0)
        gz[...] = df[...] + jnp.where(iota(back.shape, 1) < PDIM, back, 0.0)


def place(value, keep, send, start):
    half, columns = value.shape[0] // 2, slice(start, start + value.shape[1])
    keep[:, columns] = value[:half]
    send[:, columns] = value[half:]


def summed(one, two):
    return sum(dot(x[...], y[...], 0, 0) for x, y in zip(one, two))


def ff_grad_kernel(count, *refs):
    a2, dupper, dh2, hidden, a3, dy = (refs[j * count : (j + 1) * count] for j in range(6))
    keep, send, head = refs[6 * count :]
    up = summed(a2, dupper).astype(low)
    place(up, keep, send, 0)
    place(summed(dh2, hidden).astype(low), keep, send, up.shape[1])
    head[...] = summed(a3, dy).astype(low)


def attend_grad_kernel(plan, count, *refs):
    a1, dqkv, dh1, ctx = (refs[j * count : (j + 1) * count] for j in range(4))
    keep, send = refs[4 * count :]
    start = plan.qkv_at - plan.out_at
    out = summed(dh1, ctx).astype(low)
    place(jnp.pad(out, ((0, 0), (0, start - plan.d_out))), keep, send, 0)
    qkv = summed(a1, dqkv).astype(low)
    blank = plan.width - plan.qkv_at - plan.qkv
    place(jnp.pad(qkv, ((0, 0), (0, blank))), keep, send, start)


def table_grad_kernel(plan, flip, count, first_image, *refs):
    dh0, f = refs[:count], refs[count : 2 * count]
    dgains, head, keep, send = refs[2 * count :]
    shape = (8, plan.table_w)
    spot = (iota(shape, 1) == plan.gain_at + iota(shape, 0)).astype(low)
    table = dot(dgains[...].astype(low), spot, 0, 0)
    for k in range(count):
        left = left_operand(plan, flip, f[k][...], first_image[0] + k)
        table = table + dot(dh0[k][...], left, 0, 0)
    place(table.astype(low), keep, send, 0)
    place(head[...], keep, send, plan.head_at)


def join_kernel(one, two, out):
    half = one.shape[0]
    out[:half] = one[...]
    out[half:] = two[...]


def square_kernel(plan, n_mp, gp, fp, spots, qkv, out, up, down, head, table, gains, sq):
    hid = up.shape[1]
    g = gp[:, plan.qkv_at : plan.qkv_at + plan.qkv].astype(wide)
    qkv[...] = g
    total = jnp.sum(g * g)
    turn = (iota((plan.d_out, plan.d_out), 0) == iota((plan.d_out, plan.d_out), 1)).astype(low)
    g = dot(turn, gp[:, plan.out_at : plan.out_at + plan.d_out], 1, 1)
    out[...] = g
    total = total + jnp.sum(g * g)
    for source, target in ((fp[:, :hid], up), (fp[:, hid:], down)):
        g = source.astype(wide)
        target[...] = g
        total = total + jnp.sum(g * g)
    g = gp[:, plan.head_at : plan.head_at + plan.d_head].astype(wide)
    head[...] = g
    copied = jnp.sum(g * g)
    packed = gp[:, : plan.table_w]
    width = table.shape[1]
    pick = (spots[...] == iota((plan.table_w, width), 1)).astype(low)
    g = dot(packed, pick, 1, 0)
    table[...] = g
    copied = copied + jnp.sum(g * g)
    shape = (8, plan.table_w)
    spot = (iota(shape, 1) == plan.gain_at + iota(shape, 0)) & (iota(shape, 0) < 3)
    g = dot(spot.astype(low), packed, 1, 1)
    gains[...] = g[:3]
    copied = copied + jnp.sum(g * g)
    sq[0, 0] = total + copied / n_mp


def adam_step(g, w, m, v, factor, fix_one, fix_two, rate, decay):
    clipped = g * factor
    first = beta_one * m + (1.0 - beta_one) * clipped
    second = beta_two * v + (1.0 - beta_two) * clipped * clipped
    step = first / fix_one / (jnp.sqrt(second / fix_two) + adam_eps)
    return w - rate * (step + decay * w), first, second


def adam_kernel(scalars, *refs):
    factor, fix_one, fix_two = scalars[0], scalars[1], scalars[2]
    ins, outs = refs[:24], refs[24:]
    for which in range(6):
        g, w, m, v = ins[4 * which : 4 * which + 4]
        w_out, m_out, v_out = outs[3 * which : 3 * which + 3]
        values = (g[...], w[...], m[...], v[...])
        w_out[...], m_out[...], v_out[...] = adam_step(
            *values, factor, fix_one, fix_two, learn_rate, decay_rate
        )


def swap(x, axis, bit):
    return lax.ppermute(x, axis, [(j, j ^ bit) for j in range(lax.axis_size(axis))])


def swap_cores(x):
    return swap(x, "section", 1)


def mp_sum(part, turn):
    if lax.axis_size("mp") != 4:
        part = lax.psum(part, "mp")
        return part, jnp.zeros_like(part)
    bits = (1, 2) if turn % 2 == 0 else (2, 1)
    part = (part.astype(wide) + swap(part, "mp", bits[0]).astype(wide)).astype(low)
    return part, swap(part, "mp", bits[1])


def slots(x, axis):
    size = lax.axis_size(axis)
    if size > 4:
        return lax.all_gather(x, axis, axis=0)
    mine = lax.dynamic_update_slice_in_dim(
        jnp.zeros((size,) + x.shape, x.dtype), x[None], lax.axis_index(axis), 0
    )
    total = mine
    for by in range(1, size):
        total = total + lax.ppermute(mine, axis, [(j, (j + by) % size) for j in range(size)])
    return total


def everywhere_sum(vector):
    for axis in ("section", "mp", "dp"):
        vector = jnp.sum(slots(vector, axis), 0)
    return vector


def pad_columns(x, width):
    return jnp.pad(x, ((0, 0), (0, width - x.shape[1])))


def local(
    images,
    noise,
    labels,
    drop_mask,
    step_count,
    qkv_weight,
    attn_out_weight,
    up_weight,
    down_weight,
    head_weight,
    embed_table,
    gains,
    qkv_first,
    attn_out_first,
    up_first,
    down_first,
    head_first,
    embed_first,
    gains_first,
    qkv_second,
    attn_out_second,
    up_second,
    down_second,
    head_second,
    embed_second,
    gains_second,
):
    masters = (qkv_weight, attn_out_weight, up_weight, down_weight, head_weight, embed_table, gains)
    firsts = (qkv_first, attn_out_first, up_first, down_first, head_first, embed_first, gains_first)
    seconds = (
        qkv_second,
        attn_out_second,
        up_second,
        down_second,
        head_second,
        embed_second,
        gains_second,
    )
    section = lax.axis_index("section")
    n_dp = lax.axis_size("dp")
    n_mp = lax.axis_size("mp")
    here, patches = images.shape[0], images.shape[1]
    mine = here // 2
    n_img = here * n_dp
    patch_count = n_img * patches
    fixed = PDIM + patches
    classes = embed_table.shape[1] - fixed
    model = embed_table.shape[2] * n_dp
    hid = up_weight.shape[2]
    plan = Plan(
        patches,
        n_img,
        classes,
        head_weight.shape[2],
        qkv_weight.shape[2],
        attn_out_weight.shape[1],
    )

    tags = slots(jnp.where(drop_mask == 1, NCLASS, labels), "dp").reshape(n_img)
    table_t = embed_table[0].T.astype(low)
    ids = fixed + tags
    hot = (ids[:, None] == iota((n_img, fixed + classes), 1)).astype(low)
    class_t = dot(table_t, hot, 1, 1).astype(low)
    gains_t = pad_columns(gains[0].T.astype(low), 8)
    packets = (
        jnp.concatenate(
            [
                pad_columns(
                    jnp.concatenate([table_t[:, :fixed], gains_t, class_t], 1), plan.table_w
                ),
                pad_columns(head_weight[0].astype(low), plan.out_at - plan.head_at),
                pad_columns(attn_out_weight[0].T.astype(low), plan.qkv_at - plan.out_at),
                pad_columns(qkv_weight[0].astype(low), plan.width - plan.qkv_at),
            ],
            1,
        ),
        jnp.concatenate([up_weight[0].astype(low), down_weight[0].T.astype(low)], 1),
    )

    def spread(packet):
        rows = packet.shape[0] // 2
        low_rows, high_rows = packet[:rows], packet[rows:]
        moved = swap_cores(jnp.where(section == 0, high_rows, low_rows))
        return jnp.where(section == 0, low_rows, moved), jnp.where(section == 0, moved, high_rows)

    spread_packets = [spread(packet) for packet in packets]

    def gather(packet, block, tokens=()):
        own_rows = lax.all_gather(spread_packets[packet][block], "dp", axis=0, tiled=True)
        if tokens:
            own_rows = gate(own_rows, tokens)
        other = swap_cores(own_rows)
        rows, width = own_rows.shape
        out = call(join_kernel, "join", [], [own_rows, other], [((2 * rows, width), low, True)])
        return out[0]

    def gain_rows(pw):
        shape = (8, plan.table_w)
        spot = (iota(shape, 1) == plan.gain_at + iota(shape, 0)) & (iota(shape, 0) < 3)
        return dot(spot.astype(low), pw[:, : plan.table_w], 1, 1)

    def own_images(x):
        return lax.dynamic_slice_in_dim(x, section * mine, mine, 0)

    inputs = own_images(images) + noise_scale * own_images(noise)
    inputs = jnp.pad(inputs, ((0, 0), (0, 0), (0, LANES - PDIM)))
    latents = [inputs[k] for k in range(mine)]
    first_image = lax.axis_index("dp") * here + section * mine
    full = (patches, model)
    tile = (patches, LANES)
    mac = 2 * patches * model
    loss_part = 0.0
    kept = []
    turns = itertools.count()

    def exchange(part):
        return mp_sum(part, next(turns))

    def stay(x, keep):
        return near(x) if keep else x

    def sent(saved):
        return [s["p"][1] for s in saved[:-1]] + [saved[-1]["p"][0]]

    weights = []
    for block in range(2):
        pw = gather(0, block, sent(kept[0]) if block else ())
        rows = gain_rows(pw)
        flip = block == 1
        saved = []
        before = []
        for k in range(mine):
            h0, qkv, part = call(
                functools.partial(enter_kernel, plan, flip),
                "enter",
                [(first_image + k)[None].astype(ints)],
                [latents[k], near(pw), rows],
                [
                    (full, wide, False),
                    ((patches, plan.qkv), low, False),
                    (full, low, True),
                ],
                mac * (plan.table_w + plan.qkv + plan.d_out),
                patches * patches * 4,
                after=before,
            )
            before = [part]
            saved.append(dict(f=latents[k], h0=h0, qkv=qkv, p=exchange(part)))
        fw = gather(1, block, sent(saved))
        weights.append((pw, fw, rows))
        for k, kept_k in enumerate(saved):
            h1, a2, upper, part = call(
                ff_kernel,
                "ff",
                [],
                [kept_k["h0"], *map(near, kept_k["p"]), near(fw), rows],
                [
                    (full, wide, flip),
                    (full, low, flip),
                    ((patches, hid), wide, flip),
                    (full, low, True),
                ],
                mac * hid * 2,
                patches * hid,
                after=before,
            )
            before = [part]
            kept_k.update(h1=h1, a2=a2, upper=upper, p=exchange(part))
        for kept_k in saved:
            h2, scale, z, sums = call(
                functools.partial(head_kernel, plan, flip),
                "head",
                [],
                [stay(kept_k["h1"], flip), *map(near, kept_k["p"]), kept_k["f"], near(pw), rows],
                [
                    (full, wide, flip),
                    (tile, wide, False),
                    (tile, wide, False),
                    ((2, LANES), wide, False),
                ],
                mac * LANES,
                patches * LANES,
            )
            kept_k.update(h2=h2, scale=scale, z=z)
            loss_part = loss_part + jnp.sum(sums[0])
            if block == 1:
                loss_part = loss_part + 0.5 * jnp.sum(sums[1])
        latents = [kept_k["z"] for kept_k in saved]
        kept.append(saved)

    grads_z = [None] * mine
    scattered = [None, None]

    def core_sum(keep, send):
        return (keep.astype(wide) + swap_cores(send).astype(wide)).astype(low)

    def scatter(both):
        return lax.psum_scatter(both, "dp", scatter_dimension=0, tiled=True)

    for block in (1, 0):
        pw, fw, rows = weights[block]
        flip = block == 1
        saved = kept[block]
        before = []
        for k in range(mine):
            s = saved[k]
            df, dy, a3, hidden, dh2, dh2_low, dupper, part, dg2 = call(
                functools.partial(head_back_kernel, plan, flip, block == 1, float(patch_count)),
                "head_back",
                [],
                ([] if block == 1 else [grads_z[k]])
                + [s["z"], s["scale"], stay(s["h2"], flip), stay(s["upper"], flip)]
                + [near(pw), near(fw), rows],
                [
                    (tile, wide, False),
                    (tile, low, True),
                    (full, low, True),
                    ((patches, hid), low, True),
                    (full, wide, False),
                    (full, low, True),
                    ((patches, hid), low, True),
                    (full, low, True),
                    ((1, model), wide, False),
                ],
                mac * (LANES + 2 * hid),
                patches * hid,
                after=before,
            )
            before = [part]
            s.update(df=df, dy=dy, a3=a3, hidden=hidden, dh2=dh2, dh2_low=dh2_low)
            s.update(dupper=dupper, dg2=dg2, p=exchange(part))
        names = ("a2", "dupper", "dh2_low", "hidden", "a3", "dy")
        keep, send, head_grad = call(
            functools.partial(ff_grad_kernel, mine),
            "ff_grad",
            [],
            [stay(s[name], flip or name != "a2") for name in names for s in saved],
            [((model // 2, 2 * hid), low, True)] * 2 + [((model, LANES), low, True)],
            mac * hid * 2 * mine,
            grant=LARGE_GRANT,
        )
        before = before + [keep]
        ff_sum = core_sum(keep, send)
        scattered_ff = scatter(ff_sum)
        for k in range(mine):
            s = saved[k]
            dh1, dh1_low, a1, ctx, dqkv, part, dg1 = call(
                functools.partial(attend_back_kernel, plan, flip),
                "attend_back",
                [],
                [s["dh2"], *map(near, s["p"]), stay(s["h1"], flip), s["h0"], s["qkv"]]
                + [near(pw), rows],
                [
                    (full, wide, False),
                    (full, low, False),
                    (full, low, False),
                    ((patches, plan.d_out), low, False),
                    ((patches, plan.qkv), low, False),
                    (full, low, True),
                    ((1, model), wide, False),
                ],
                mac * (plan.d_out * 2 + plan.qkv),
                patches * patches * 4,
                after=before + ([ff_sum] if k == 1 else []),
            )
            before = [part]
            s.update(dh1=dh1, dh1_low=dh1_low, a1=a1, ctx=ctx, dqkv=dqkv, dg1=dg1)
            s.update(p=exchange(part))
        keep, send = call(
            functools.partial(attend_grad_kernel, plan, mine),
            "attend_grad",
            [],
            [s[name] for name in ("a1", "dqkv", "dh1_low", "ctx") for s in saved],
            [((model // 2, plan.width - plan.out_at), low, True)] * 2,
            mac * (plan.width - plan.out_at) * mine,
            grant=LARGE_GRANT,
        )
        attend_sum = core_sum(keep, send)
        for k in range(mine):
            s = saved[k]
            outs = call(
                functools.partial(leave_back_kernel, plan, block == 1),
                "leave_back",
                [],
                [s["dh1"], *map(near, s["p"]), s["h0"], rows]
                + ([s["df"], near(pw)] if block == 1 else []),
                [(full, low, True), ((1, model), wide, False)]
                + ([(tile, wide, False)] if block == 1 else []),
                mac * LANES,
                after=[keep] if k == 0 else [],
            )
            s.update(dh0=outs[0], dg0=outs[1])
            if block == 1:
                grads_z[k] = outs[2]
        dgains = jnp.concatenate(
            [sum(s[name] for s in saved) for name in ("dg0", "dg1", "dg2")]
            + [jnp.zeros((5, model), wide)],
            0,
        )
        keep, send = call(
            functools.partial(table_grad_kernel, plan, flip, mine),
            "table_grad",
            [first_image[None].astype(ints)],
            [near(s["dh0"]) for s in saved] + [s["f"] for s in saved] + [dgains, near(head_grad)],
            [((model // 2, plan.out_at), low, True)] * 2,
            mac * plan.table_w * mine,
            grant=LARGE_GRANT,
        )
        table_sum = core_sum(keep, send)
        scattered[block] = (
            scatter(jnp.concatenate([table_sum, attend_sum], 1)),
            scattered_ff,
        )

    own = []
    for at in range(2):
        zero, one = scattered[0][at], scattered[1][at]
        moved = swap_cores(jnp.where(section == 0, one, zero))
        own.append(
            jnp.where(
                section == 0,
                jnp.concatenate([zero, moved], 0),
                jnp.concatenate([moved, one], 0),
            )
        )

    spots = jnp.concatenate(
        [
            jnp.arange(fixed, dtype=ints),
            jnp.full((8,), -1, ints),
            ids.astype(ints),
            jnp.full((plan.table_w - plan.class_at - n_img,), -1, ints),
        ]
    )[:, None]

    def flat(x, which):
        return x[0].T if which in (3, 5) else x[0]

    shapes = [flat(w, which).shape for which, w in enumerate(masters)]
    *grads, squares = pl.pallas_call(
        functools.partial(square_kernel, plan, float(n_mp)),
        out_shape=[jax.ShapeDtypeStruct(s, wide) for s in shapes]
        + [jax.ShapeDtypeStruct((1, 1), wide)],
        out_specs=[pl.BlockSpec(memory_space=pltpu.VMEM)] * 7
        + [pl.BlockSpec(memory_space=pltpu.SMEM)],
        name="squares",
        compiler_params=pltpu.CompilerParams(vmem_limit_bytes=LARGE_GRANT),
    )(*own, spots)

    summed = everywhere_sum(jnp.stack([squares[0, 0], loss_part / (patch_count * n_mp)]))
    grad_norm = jnp.sqrt(summed[0])
    param_count = 2 * sum(
        masters[which].size * n_dp * (n_mp if which < 4 else 1) for which in range(7)
    )
    limit = clip_scale * math.sqrt(param_count / patch_count)
    factor = jnp.minimum(1.0, limit / grad_norm)
    steps_done = step_count[0].astype(wide)
    fix_one = 1.0 - beta_one**steps_done
    fix_two = 1.0 - beta_two**steps_done
    arrays = []
    for which in range(6):
        arrays.append(grads[which])
        arrays += [flat(x[which], which) for x in (masters, firsts, seconds)]
    fresh = call(
        adam_kernel,
        "adam",
        [jnp.stack([factor, fix_one, fix_two])],
        arrays,
        [(shapes[which], wide, False) for which in range(6) for _ in range(3)],
        grant=LARGE_GRANT,
    )
    results = [summed[1], grad_norm]
    for at, x in enumerate(fresh):
        results.append((x.T if at // 3 in (3, 5) else x)[None])
    results += adam_step(
        grads[6][None], gains, gains_first, gains_second, factor, fix_one, fix_two, gain_rate, 0.0
    )
    return tuple(results)


def solution(mesh):
    split_rows = P("section", "dp", "mp")
    split_columns = P("section", "mp", "dp")
    weights = (
        split_rows,
        split_columns,
        split_rows,
        split_columns,
        P("section", "dp", None),
        P("section", None, "dp"),
        P("section", None, "dp"),
    )
    return jax.shard_map(
        local,
        mesh=mesh,
        in_specs=(P("dp", None, None), P("dp", None, None), P("dp"), P("dp"), P()) + weights * 3,
        out_specs=(P(), P()) + tuple(spec for spec in weights for _ in range(3)),
        check_vma=False,
    )
```
